32 devices in a mesh: cam: 4 (over y, x), dev: 8 (over z, core).
Axes of the slice: x: 2, y: 2, z: 4, core: 2. Of those that a mesh axis runs over, the one named last changes fastest.
Arguments:
- params: float32 [256, 59, 128], P('dev'), may hold values from -4 to 4
- moment_first: float32 [8, 4, 8, 59, 128], P('dev', 'cam'), may hold values from -3 to 3
- moment_second: float32 [8, 4, 8, 59, 128], P('dev', 'cam'), may hold values from 0.01 to 1
- cam_proj: float32 [8, 9, 59], P('cam'), may hold values from -0.75 to 0.75
- send_block: int32 [8, 8, 8, 2], P('cam', 'dev'), may hold values from 0 to 31
- tile_slot: int32 [8, 16, 8], P('cam', 'dev'), may hold values from 0 to 15, as said below
- tile_count: int32 [8, 16], P('cam', 'dev'), may hold values from 2 to 8, as said below
- targets: float32 [8, 16, 3, 256], P('cam', 'dev'), may hold values from 0 to 1
- split_block: int32 [8, 8], P('dev'), may hold values from 0 to 31, as said below
- split_live: int32 [8, 8], P('dev'), may hold values from 0 to 1, as said below
Outputs:
- images: float32 [8, 16, 3, 256], P('cam', 'dev')
- new_params: float32 [256, 59, 128], P('dev')
- new_first: float32 [8, 4, 8, 59, 128], P('dev', 'cam')
- new_second: float32 [8, 4, 8, 59, 128], P('dev', 'cam')
- children: float32 [64, 2, 59, 128], P('dev')
The draws below stay inside these ranges and needn't reach their ends.
Inputs may be any that keep to these rules, and one draw needn't show every extreme that they name: `tile_count`: in every camera some tile has exactly 8 live entries. `tile_slot`: the entries of one tile's list are distinct; entries at positions from the tile's count on are not read. `split_block`: among an owner's entries where split_live is 1 the blocks are distinct. `split_live`: each row holds exactly 2 ones; in every draw some new owner has a one in every row.
All inputs are finite; a program needn't handle non-finite values.
Results may differ from the reference program's by a relative error of at most 0.0003.
Values sent between devices are 32-bit elements; how exact they have to be, the bound alone decides.
A program may use at most 64 MiB of HBM per device.

```python
import math
import jax
import jax.numpy as jnp
from jax import lax

F = 59
SPL = 128
TSIDE = 16
PIX = 256
PROJ = 9
KMAX = 8
BLK_DEV = 32
TILE_DEV = 2
OWNERS = 8
GROUPS = 4
CAMERAS = 8
TILES = 16
NBLK = 256
BQ = 8
CAP = 2
SLOTS = 16
SPLIT_DEV = 2


def depth_lists(key):
    folded = jax.random.fold_in(key, 7101)
    key_level, key_heavy, key_count, key_order = jax.random.split(folded, 4)
    load_level = jax.random.randint(key_level, (CAMERAS, OWNERS), max(1, KMAX // 2), KMAX + 1)
    heavy_owner = jax.random.randint(key_heavy, (CAMERAS, 1), 0, OWNERS)
    owner_ids = jnp.arange(OWNERS, dtype=jnp.int32)[None, :]
    load_level = jnp.where(owner_ids == heavy_owner, KMAX, load_level)
    lowest = jnp.maximum(load_level // 2, 1)
    tile_counts = jax.random.randint(key_count, (CAMERAS, OWNERS, TILE_DEV), lowest[:, :, None], load_level[:, :, None] + 1)
    first_tile = jnp.arange(TILE_DEV, dtype=jnp.int32)[None, None, :] == 0
    tile_counts = jnp.where((owner_ids[:, :, None] == heavy_owner[:, :, None]) & first_tile, KMAX, tile_counts)
    tile_counts = tile_counts.reshape(CAMERAS, TILES).astype(jnp.int32)
    scores = jax.random.randint(key_order, (CAMERAS, TILES, SLOTS), 0, 1 << 20) * SLOTS + jnp.arange(SLOTS, dtype=jnp.int32)
    slot_order = jnp.argsort(scores, axis=-1)[:, :, :KMAX].astype(jnp.int32)
    return (slot_order, tile_counts)


def draw_tile_slot(key, part):
    return depth_lists(key)[0]


def draw_tile_count(key, part):
    return depth_lists(key)[1]


def split_plan(key):
    folded = jax.random.fold_in(key, 7202)
    key_popular, key_target, key_rank, key_block = jax.random.split(folded, 4)
    popular = jax.random.randint(key_popular, (OWNERS,), 0, 4)
    favoured = jax.random.randint(key_target, (), 0, OWNERS)
    owner_ids = jnp.arange(OWNERS, dtype=jnp.int32)
    popular = jnp.where(owner_ids == favoured, 4, popular)
    scores = (popular[None, :] * (1 << 16) + jax.random.randint(key_rank, (OWNERS, OWNERS), 0, 1 << 16)) * OWNERS + owner_ids[None, :]
    dest_rank = jnp.argsort(jnp.argsort(-scores, axis=1), axis=1).astype(jnp.int32)
    live_mask = (dest_rank < SPLIT_DEV).astype(jnp.int32)
    block_scores = jax.random.randint(key_block, (OWNERS, BLK_DEV), 0, 1 << 20) * BLK_DEV + jnp.arange(BLK_DEV, dtype=jnp.int32)[None, :]
    blocks = jnp.argsort(block_scores, axis=1).astype(jnp.int32)
    chosen = jnp.take_along_axis(blocks, dest_rank % BLK_DEV, axis=1)
    return (chosen.astype(jnp.int32), live_mask)


def draw_split_block(key, part):
    return split_plan(key)[0]


def draw_split_live(key, part):
    return split_plan(key)[1]


def set_ends(array, own_key, low, high):
    shape = array.shape
    index_at = [jax.random.randint(jax.random.fold_in(own_key, axis), (), 0, shape[axis]) for axis in range(len(shape))]
    array = array.at[tuple(index_at)].set(low)
    longest = shape.index(max(shape))
    index_at[longest] = (index_at[longest] + 1) % shape[longest]
    return array.at[tuple(index_at)].set(high)


def steps_of(rng, extent, shards, smallest, high):
    gain, own = 1.0, jax.random.fold_in(rng, 6)
    for position, blocks in shards:
        heights = jnp.exp(jax.random.uniform(jax.random.fold_in(own, position), (blocks,), jnp.float32, smallest / len(shards), high / len(shards)))
        gain = gain * jnp.repeat(heights, extent[position] // blocks).reshape([-1 if axis == position else 1 for axis in range(len(extent))])
    return gain


def centred(rng, dims, deviation, reach, cuts=(), kind=jnp.bfloat16):
    result = deviation * jax.random.normal(rng, dims, jnp.float32)
    if cuts:
        result = result * steps_of(rng, dims, cuts, -0.22, 0.18)
    return jnp.clip(result, -reach, reach).astype(kind)


def setup_inputs(seed: int = 0) -> dict:
    streams_of = jax.random.split(jax.random.key(seed), 11)
    params = centred(streams_of[0], (NBLK, F, SPL), 1.0, 4.0, ((0, 8),), jnp.float32)
    moment_first = centred(streams_of[1], (OWNERS, GROUPS, BQ, F, SPL), 0.5, 3.0, ((0, 8), (1, 4)), jnp.float32)
    moment_second = jnp.clip(jnp.exp(math.log(1.0) - 4.6051702 * jax.random.uniform(streams_of[2], (OWNERS, GROUPS, BQ, F, SPL), jnp.float32) ** steps_of(streams_of[2], (OWNERS, GROUPS, BQ, F, SPL), ((0, 8), (1, 4)), -0.2, 0.2)), 0.01, 1.0)
    cam_proj = centred(streams_of[3], (CAMERAS, PROJ, F), F ** -0.5, 0.75, ((0, 4),), jnp.float32)
    send_block = set_ends(jax.random.randint(streams_of[4], (CAMERAS, OWNERS, OWNERS, CAP), 0, BLK_DEV), jax.random.fold_in(streams_of[4], 1), 0, BLK_DEV - 1).astype(jnp.int32)
    tile_slot = draw_tile_slot(jax.random.fold_in(streams_of[10], 71), 0)
    tile_count = draw_tile_count(jax.random.fold_in(streams_of[10], 71), 0)
    targets = jnp.clip(1.0 * jax.random.uniform(streams_of[7], (CAMERAS, TILES, 3, PIX), jnp.float32) ** steps_of(streams_of[7], (CAMERAS, TILES, 3, PIX), ((0, 4), (1, 8)), -0.2, 0.2), 0.0, 1.0)
    split_block = draw_split_block(jax.random.fold_in(streams_of[10], 71), 0)
    split_live = draw_split_live(jax.random.fold_in(streams_of[10], 71), 0)
    return {"params": params, "moment_first": moment_first, "moment_second": moment_second, "cam_proj": cam_proj, "send_block": send_block, "tile_slot": tile_slot, "tile_count": tile_count, "targets": targets, "split_block": split_block, "split_live": split_live}


LOSS_WEIGHT = 256.0
RATE = 0.01
BETA_FIRST = 0.9
BETA_SECOND = 0.999
EPSILON = 1e-08
SHRINK = math.log(1.6)
PRECISE = lax.Precision.HIGHEST

def unpack(projected):
    centre = 0.5 * TSIDE
    spread = 0.375 * TSIDE
    mean_x = centre + spread * jnp.tanh(projected[:, 0])
    mean_y = centre + spread * jnp.tanh(projected[:, 1])
    conic_a = 0.02 + 0.1 * jax.nn.softplus(projected[:, 2])
    conic_c = 0.02 + 0.1 * jax.nn.softplus(projected[:, 4])
    conic_b = 0.9 * jnp.sqrt(conic_a * conic_c) * jnp.tanh(projected[:, 3])
    opacity = 0.99 * jax.nn.sigmoid(projected[:, 5] - 6.0)
    shape_part = jnp.stack([mean_x, mean_y, conic_a, conic_b, conic_c, opacity], axis=1)
    return jnp.concatenate([shape_part, jax.nn.sigmoid(projected[:, 6:9])], axis=1)

def project(params, matrix):
    projected = jnp.einsum('pf,bfs->bps', matrix, params, precision=PRECISE)
    return unpack(projected)

def footprint(features, active, grid_x, grid_y):
    off_x = grid_x[None, None, :] - features[:, 0, :, None]
    off_y = grid_y[None, None, :] - features[:, 1, :, None]
    exponent = 0.5 * (features[:, 2, :, None] * off_x * off_x + 2.0 * features[:, 3, :, None] * off_x * off_y + features[:, 4, :, None] * off_y * off_y)
    falloff = jnp.exp(-exponent) * active[:, None, None]
    alpha_term = features[:, 5, :, None] * falloff
    return (off_x, off_y, falloff, alpha_term)

def divide(parents):
    offset = 0.5 * jnp.exp(parents[:, 3:6] - 1.0)
    shrunk = parents[:, 3:6] - SHRINK
    remainder = parents[:, 6:]
    child_plus = jnp.concatenate([parents[:, 0:3] + offset, shrunk, remainder], axis=1)
    child_minus = jnp.concatenate([parents[:, 0:3] - offset, shrunk, remainder], axis=1)
    return jnp.stack([child_plus, child_minus], axis=1)

def reference(params, moment_first, moment_second, cam_proj, send_block, tile_slot, tile_count, targets, split_block, split_live):
    pixel_ids = jnp.arange(TSIDE * TSIDE, dtype=jnp.int32)
    grid_x = (pixel_ids % TSIDE).astype(jnp.float32) + 0.5
    grid_y = (pixel_ids // TSIDE).astype(jnp.float32) + 0.5
    owner_ids = jnp.arange(TILES, dtype=jnp.int32) // TILE_DEV
    source_ids = (tile_slot // CAP).astype(jnp.int32)
    within_ids = (tile_slot % CAP).astype(jnp.int32)
    camera_ids = jnp.arange(CAMERAS, dtype=jnp.int32)[:, None, None]
    block_of = (source_ids * BLK_DEV + send_block[camera_ids, source_ids, owner_ids[None, :, None], within_ids]).astype(jnp.int32)
    live_rows = (jnp.arange(KMAX, dtype=jnp.int32)[None, None, :] < tile_count[:, :, None]).astype(jnp.float32)

    def tile_group(features_all, group_blocks, group_live):

        def advance(state_carry, inputs):
            transmit, colour = state_carry
            blocks_now, live_now = inputs
            features = jnp.take(features_all, blocks_now, axis=0)
            unused_x, unused_y, unused_fall, alpha_term = footprint(features, live_now, grid_x, grid_y)
            log_keep = jnp.log1p(-alpha_term)
            log_before = jnp.cumsum(log_keep, axis=1) - log_keep
            weights = alpha_term * transmit[:, None, :] * jnp.exp(log_before)
            colour = colour + jnp.einsum('dcs,dsp->dcp', features[:, 6:9], weights, precision=PRECISE)
            transmit = transmit * jnp.exp(lax.optimization_barrier(jnp.sum(log_keep, axis=1)))
            return ((transmit, colour), None)
        tile_rows = group_blocks.shape[0]
        start_state = (jnp.ones((tile_rows, PIX), jnp.float32), jnp.zeros((tile_rows, 3, PIX), jnp.float32))
        scanned = lax.scan(jax.checkpoint(advance), start_state, (group_blocks.T, group_live.T))
        return scanned[0][1]

    def loss_all(values):

        def per_camera(inputs):
            matrix, blocks_cam, live_cam, target_cam = inputs
            features_all = project(values, matrix)

            def per_group(group_data):
                return tile_group(features_all, group_data[0], group_data[1])
            grouped = lax.map(jax.checkpoint(per_group), (blocks_cam.reshape(OWNERS, TILE_DEV, KMAX), live_cam.reshape(OWNERS, TILE_DEV, KMAX)))
            colour = grouped.reshape(TILES, 3, PIX)
            error = colour - target_cam
            return (0.5 * LOSS_WEIGHT * jnp.sum(error * error), colour)
        losses, colours = lax.map(jax.checkpoint(per_camera), (cam_proj, block_of, live_rows, targets))
        return (jnp.sum(losses), colours)
    gradient, images = jax.grad(loss_all, has_aux=True)(params)
    first_moment = moment_first.reshape(params.shape)
    second_moment = moment_second.reshape(params.shape)
    new_first = BETA_FIRST * first_moment + (1.0 - BETA_FIRST) * gradient
    new_second = BETA_SECOND * second_moment + (1.0 - BETA_SECOND) * gradient * gradient
    new_params = params - RATE * new_first / (jnp.sqrt(new_second) + EPSILON)
    parent_ids = (jnp.arange(OWNERS, dtype=jnp.int32)[None, :] * BLK_DEV + split_block.T).astype(jnp.int32)
    live_mask = split_live.T.reshape(-1).astype(jnp.float32)
    parents = jnp.take(new_params, parent_ids.reshape(-1), axis=0)
    children = divide(parents) * live_mask[:, None, None, None]
    return (images, new_params, new_first.reshape(moment_first.shape), new_second.reshape(moment_second.shape), children)
```

```python
import functools
import math

import jax
import jax.numpy as jnp
from jax import lax
from jax.experimental import pallas as pl
from jax.experimental.pallas import tpu as pltpu
from jax.sharding import PartitionSpec as P

TSIDE = 16
PROJ = 9
LOSS_WEIGHT = 256.0
RATE = 0.01
BETA_FIRST = 0.9
BETA_SECOND = 0.999
EPSILON = 1e-08
SHRINK = math.log(1.6)
LOG2E = math.log2(math.e)
MESH = pl.DeviceIdType.MESH
HIGHEST = lax.Precision.HIGHEST
F32 = jnp.float32
BF16 = jnp.bfloat16
VMEM = pl.BlockSpec(memory_space=pltpu.VMEM)
SMEM = pl.BlockSpec(memory_space=pltpu.SMEM)
BIG = 60 * 1024 * 1024


def split2(value):
    high = value.astype(BF16)
    return high, (value - high.astype(F32)).astype(BF16)


def dot32(left, right, dims=(((1,), (0,)), ((), ()))):
    return lax.dot_general(left, right, dims, preferred_element_type=F32)


def softplus(value):
    return jnp.maximum(value, 0.0) + jnp.log(1.0 + jnp.exp(-jnp.abs(value)))


def sigmoid(value):
    return 1.0 / (1.0 + jnp.exp(-value))


def project_kernel(send_ref, matrix_ref, params_ref, out_ref, rows_ref):
    owned = params_ref.shape[0]
    cameras, _, owners, cap = send_ref.shape
    matrix = matrix_ref[...]
    for block in range(owned):
        rows_ref[block] = jnp.dot(matrix, params_ref[block], precision=HIGHEST, preferred_element_type=F32)
    for owner in range(owners):
        for camera in range(cameras):
            for place in range(cap):
                chosen = send_ref[camera, 0, owner, place]
                first = (camera * cap + place) * PROJ
                out_ref[owner, first : first + PROJ, :] = rows_ref[
                    chosen, camera * 16 : camera * 16 + PROJ, :
                ]


def exchange_kernel(axis, count, x_ref, out_ref, land, send_sems, recv_sems):
    me = lax.axis_index(axis)
    barrier = pltpu.get_barrier_semaphore()
    for step in range(1, count):
        pl.semaphore_signal(
            barrier, inc=1, device_id={axis: lax.rem(me + step, count)}, device_id_type=MESH
        )
    pl.semaphore_wait(barrier, count - 1)
    copies = []
    for step in range(1, count):
        peer = lax.rem(me + step, count)
        copy = pltpu.make_async_remote_copy(
            src_ref=x_ref.at[peer],
            dst_ref=land.at[me],
            send_sem=send_sems.at[step - 1],
            recv_sem=recv_sems.at[step - 1],
            device_id={axis: peer},
            device_id_type=MESH,
        )
        copy.start()
        copies.append(copy)
    out_ref[me] = x_ref[me]
    for step in range(1, count):
        copies[step - 1].wait_recv()
        source = lax.rem(me - step + count, count)
        out_ref[source] = land[source]
    for copy in copies:
        copy.wait_send()


def exchange(x, axis, ident):
    count = x.shape[0]
    return pl.pallas_call(
        functools.partial(exchange_kernel, axis, count),
        out_shape=jax.ShapeDtypeStruct(x.shape, F32),
        in_specs=[VMEM],
        out_specs=VMEM,
        scratch_shapes=[
            pltpu.VMEM(x.shape, F32),
            pltpu.SemaphoreType.DMA((count - 1,)),
            pltpu.SemaphoreType.DMA((count - 1,)),
        ],
        compiler_params=pltpu.CompilerParams(
            collective_id=ident, has_side_effects=True, vmem_limit_bytes=BIG
        ),
        name=f"exchange_{ident}",
    )(x)


def return_kernel(owners, groups, x_ref, out_ref, land, zsend, zrecv, csend, crecv):
    me = lax.axis_index("dev")
    group = lax.axis_index("cam")
    barrier = pltpu.get_barrier_semaphore()
    for step in range(1, owners):
        pl.semaphore_signal(
            barrier, inc=1, device_id={"dev": lax.rem(me + step, owners)}, device_id_type=MESH
        )
    for step in range(1, groups):
        pl.semaphore_signal(
            barrier, inc=1, device_id={"cam": lax.rem(group + step, groups)}, device_id_type=MESH
        )
    pl.semaphore_wait(barrier, owners + groups - 2)
    along = []
    for step in range(1, owners):
        peer = lax.rem(me + step, owners)
        copy = pltpu.make_async_remote_copy(
            src_ref=x_ref.at[peer],
            dst_ref=land.at[0, me],
            send_sem=zsend.at[step - 1],
            recv_sem=zrecv.at[step - 1],
            device_id={"dev": peer},
            device_id_type=MESH,
        )
        copy.start()
        along.append(copy)
    across = []
    for step in range(owners):
        source = lax.rem(me - step + owners, owners)
        if step:
            along[step - 1].wait_recv()
        piece = land.at[0, source] if step else x_ref.at[me]
        for turn in range(1, groups):
            copy = pltpu.make_async_remote_copy(
                src_ref=piece,
                dst_ref=land.at[turn, source],
                send_sem=csend.at[turn - 1, step],
                recv_sem=crecv.at[turn - 1, step],
                device_id={"cam": lax.rem(group - turn + groups, groups)},
                device_id_type=MESH,
            )
            copy.start()
            across.append((turn, source, copy))
        out_ref[0, source] = land[0, source] if step else x_ref[me]
    for turn, source, copy in across:
        copy.wait_recv()
        out_ref[turn, source] = land[turn, source]
    for copy in along:
        copy.wait_send()
    for _, _, copy in across:
        copy.wait_send()


def return_home(x, groups):
    owners = x.shape[0]
    shape = (groups,) + x.shape
    return pl.pallas_call(
        functools.partial(return_kernel, owners, groups),
        out_shape=jax.ShapeDtypeStruct(shape, F32),
        in_specs=[VMEM],
        out_specs=VMEM,
        scratch_shapes=[
            pltpu.VMEM(shape, F32),
            pltpu.SemaphoreType.DMA((owners - 1,)),
            pltpu.SemaphoreType.DMA((owners - 1,)),
            pltpu.SemaphoreType.DMA((groups - 1, owners)),
            pltpu.SemaphoreType.DMA((groups - 1, owners)),
        ],
        compiler_params=pltpu.CompilerParams(
            collective_id=7, has_side_effects=True, vmem_limit_bytes=BIG
        ),
        name="return_home",
    )(x)


def shape_of(raw):
    turn_x = jnp.tanh(raw[0])
    turn_y = jnp.tanh(raw[1])
    conic_a = 0.02 + 0.1 * softplus(raw[2])
    conic_c = 0.02 + 0.1 * softplus(raw[4])
    turn_b = jnp.tanh(raw[3])
    root = jnp.sqrt(conic_a * conic_c)
    return turn_x, turn_y, conic_a, conic_c, turn_b, root


def render_kernel(
    slot_ref, count_ref, received_ref, target_ref, image_ref, back_ref,
    feats, grads, weights, pairs, ratios, carry, before, after_tri, cot_rows, cot_cols, picture,
):
    cameras, tiles, _ = slot_ref.shape
    owners, rows, splats = received_ref.shape
    cap = rows // (PROJ * cameras)
    centre = 0.5 * TSIDE
    spread = 0.375 * TSIDE
    pixels = TSIDE * TSIDE
    half = 128
    per_chunk = half // TSIDE

    feats[...] = jnp.zeros(feats.shape, F32)
    grads[...] = jnp.zeros(grads.shape, F32)
    for index in range(cameras * cap):
        raw = [received_ref[:, index * PROJ + k, :] for k in range(PROJ)]
        turn_x, turn_y, conic_a, conic_c, turn_b, root = shape_of(raw)
        conic_b = 0.9 * root * turn_b
        feats[:, index, 0, :] = centre + spread * turn_x
        feats[:, index, 1, :] = centre + spread * turn_y
        feats[:, index, 2, :] = (0.5 * LOG2E) * conic_a
        feats[:, index, 3, :] = LOG2E * conic_b
        feats[:, index, 4, :] = (0.5 * LOG2E) * conic_c
        feats[:, index, 5, :] = math.log2(0.99) - LOG2E * softplus(6.0 - raw[5])
        for k in range(3):
            feats[:, index, 8 + k, :] = sigmoid(raw[6 + k])

    row = lax.broadcasted_iota(jnp.int32, (splats, splats), 0)
    column = lax.broadcasted_iota(jnp.int32, (splats, splats), 1)
    ones = jnp.ones((splats, splats), BF16)
    lower = jnp.where(row < column, 1.0, 0.0).astype(BF16)
    upper = jnp.where(row > column, 1.0, 0.0).astype(BF16)
    for part in range(2):
        before[part * splats : (part + 1) * splats, :splats] = lower
        before[part * splats : (part + 1) * splats, splats:] = ones
        after_tri[part * splats : (part + 1) * splats, :splats] = upper
        after_tri[part * splats : (part + 1) * splats, splats:] = ones
    grid = lax.broadcasted_iota(jnp.int32, (TSIDE, splats), 0).astype(F32) + 0.5
    pad_rows = jnp.zeros((8, splats), F32)

    def entry_of(camera, tile, position):
        slot = slot_ref[camera, tile, position]
        return slot // cap, camera * cap + slot % cap

    def tile_step(number, _):
        camera = number // tiles
        tile = number % tiles
        live = count_ref[camera, tile]
        carry[...] = jnp.zeros(carry.shape, F32)
        picture[...] = jnp.zeros(picture.shape, F32)

        def forward(position, _):
            owner, index = entry_of(camera, tile, position)
            part = lambda k: feats[owner, index, k : k + 1, :]
            off_x = grid - part(0)
            off_y = grid - part(1)
            in_x = -(part(2) * off_x * off_x)
            cross = -(part(3) * off_x)
            in_y = part(5) - part(4) * off_y * off_y
            for chunk in range(pixels // half):
                where = slice(chunk * half, (chunk + 1) * half)
                lines = []
                for line in range(chunk * per_chunk, (chunk + 1) * per_chunk):
                    lines.append(in_x + (in_y[line : line + 1] + cross * off_y[line : line + 1]))
                alpha = jnp.exp2(jnp.concatenate(lines, axis=0))
                log_keep = jnp.log2(1.0 - alpha)
                summed = dot32(jnp.concatenate(split2(log_keep), axis=1), before[...])
                held = carry[where, :]
                weight = alpha * jnp.exp2(summed[:, :splats] + held)
                carry[where, :] = held + summed[:, splats:]
                weights[position, where, :] = weight
                pairs[position, where, :] = jnp.concatenate(split2(weight), axis=1)
                ratios[position, where, :] = alpha * jnp.exp2(-log_keep)
            colour_high, colour_low = split2(feats[owner, index, 8:16, :])
            colour_high = colour_high.astype(F32)
            colour_low = colour_low.astype(F32)
            shades = jnp.concatenate(
                [
                    jnp.concatenate([colour_high, colour_low], axis=0),
                    jnp.concatenate([colour_high, pad_rows], axis=0),
                ],
                axis=1,
            ).astype(BF16)
            drawn = dot32(shades, pairs[position], (((1,), (1,)), ((), ())))
            picture[...] += drawn[:8] + drawn[8:]
            return 0

        lax.fori_loop(0, live, forward, 0)
        colour = picture[0:3, :]
        image_ref[camera, tile] = colour
        picture[0:3, :] = LOSS_WEIGHT * (colour - target_ref[camera, tile])
        cot_high, cot_low = split2(picture[...])
        cot_high = cot_high.astype(F32)
        cot_low = cot_low.astype(F32)
        cot_rows[...] = jnp.concatenate([cot_high, cot_low], axis=0).astype(BF16)
        stacked = jnp.concatenate(
            [cot_high, cot_low, cot_high, jnp.zeros((half - 24, pixels), F32)], axis=0
        )
        cot_cols[...] = stacked.T.astype(BF16)
        carry[...] = jnp.zeros(carry.shape, F32)

        def backward(reverse, _):
            position = live - 1 - reverse
            owner, index = entry_of(camera, tile, position)
            part = lambda k: feats[owner, index, k : k + 1, :]
            off_x = grid - part(0)
            off_y = grid - part(1)
            colour_high, colour_low = split2(feats[owner, index, 8:16, :])
            colour_high = colour_high.astype(F32)
            shades = jnp.concatenate(
                [colour_high, colour_high, colour_low.astype(F32), jnp.zeros((half - 24, splats), F32)],
                axis=0,
            ).astype(BF16)
            total0 = jnp.zeros((TSIDE, splats), F32)
            total1 = jnp.zeros((TSIDE, splats), F32)
            total2 = jnp.zeros((TSIDE, splats), F32)
            for chunk in range(pixels // half):
                where = slice(chunk * half, (chunk + 1) * half)
                shade = dot32(cot_cols[where, :], shades)
                shaded = shade * weights[position, where, :]
                summed = dot32(jnp.concatenate(split2(shaded), axis=1), after_tri[...])
                held = carry[where, :]
                carry[where, :] = held + summed[:, splats:]
                pull = shaded - (summed[:, :splats] + held) * ratios[position, where, :]
                for line in range(per_chunk):
                    height = off_y[chunk * per_chunk + line : chunk * per_chunk + line + 1]
                    piece = pull[line * TSIDE : (line + 1) * TSIDE]
                    lifted = piece * height
                    total0 += piece
                    total1 += lifted
                    total2 += lifted * height
            sum_of = lambda value: jnp.sum(value, axis=0, keepdims=True)
            wide = total0 * off_x
            moments = jnp.concatenate(
                [
                    sum_of(total0),
                    sum_of(wide),
                    sum_of(total1),
                    sum_of(wide * off_x),
                    sum_of(total1 * off_x),
                    sum_of(total2),
                    jnp.zeros((2, splats), F32),
                ],
                axis=0,
            )
            tinted = dot32(cot_rows[...], pairs[position])
            grads[owner, index, 0:8, :] += moments
            grads[owner, index, 8:16, :] += (
                tinted[:8, :splats] + tinted[8:, :splats] + tinted[:8, splats:]
            )
            return 0

        lax.fori_loop(0, live, backward, 0)
        return 0

    lax.fori_loop(0, cameras * tiles, tile_step, 0)

    for index in range(cameras * cap):
        raw = [received_ref[:, index * PROJ + k, :] for k in range(PROJ)]
        turn_x, turn_y, conic_a, conic_c, turn_b, root = shape_of(raw)
        conic_b = 0.9 * root * turn_b
        sum0, sum_x, sum_y, sum_xx, sum_xy, sum_yy = [grads[:, index, k, :] for k in range(6)]
        grad_b = -sum_xy
        grad_a = -0.5 * sum_xx + grad_b * (0.5 * conic_b / conic_a)
        grad_c = -0.5 * sum_yy + grad_b * (0.5 * conic_b / conic_c)
        results = [
            (conic_a * sum_x + conic_b * sum_y) * (spread * (1.0 - turn_x * turn_x)),
            (conic_b * sum_x + conic_c * sum_y) * (spread * (1.0 - turn_y * turn_y)),
            grad_a * (0.1 * sigmoid(raw[2])),
            grad_b * (0.9 * root * (1.0 - turn_b * turn_b)),
            grad_c * (0.1 * sigmoid(raw[4])),
            sum0 * sigmoid(6.0 - raw[5]),
        ]
        for k in range(3):
            tone = sigmoid(raw[6 + k])
            results.append(grads[:, index, 8 + k, :] * (tone * (1.0 - tone)))
        for k in range(PROJ):
            back_ref[:, index * PROJ + k, :] = results[k]


def render(slots, counts, received, targets):
    owners, rows, splats = received.shape
    cameras, tiles, depth = slots.shape
    pixels = targets.shape[-1]
    cap = rows // (PROJ * cameras)
    return pl.pallas_call(
        render_kernel,
        out_shape=(
            jax.ShapeDtypeStruct(targets.shape, F32),
            jax.ShapeDtypeStruct(received.shape, F32),
        ),
        in_specs=[SMEM, SMEM, VMEM, VMEM],
        out_specs=(VMEM, VMEM),
        scratch_shapes=[
            pltpu.VMEM((owners, cameras * cap, 16, splats), F32),
            pltpu.VMEM((owners, cameras * cap, 16, splats), F32),
            pltpu.VMEM((depth, pixels, splats), F32),
            pltpu.VMEM((depth, pixels, 2 * splats), BF16),
            pltpu.VMEM((depth, pixels, splats), F32),
            pltpu.VMEM((pixels, splats), F32),
            pltpu.VMEM((2 * splats, 2 * splats), BF16),
            pltpu.VMEM((2 * splats, 2 * splats), BF16),
            pltpu.VMEM((16, pixels), BF16),
            pltpu.VMEM((pixels, 128), BF16),
            pltpu.VMEM((8, pixels), F32),
        ],
        compiler_params=pltpu.CompilerParams(vmem_limit_bytes=BIG),
        cost_estimate=pl.CostEstimate(
            flops=20_000_000_000, bytes_accessed=100_000_000, transcendentals=4_000_000
        ),
        name="render",
    )(slots, counts, received, targets)


def update_kernel(groups, *refs):
    send_ref, split_ref, live_ref, back_ref, matrix_ref, params_ref = refs[:6]
    firsts = refs[6 : 6 + groups]
    seconds = refs[6 + groups : 6 + 2 * groups]
    params_out, first_out, second_out, parent_out, table = refs[6 + 2 * groups :]
    me = lax.axis_index("cam")
    cameras, owners, cap = send_ref.shape[1:]
    share = firsts[0].shape[0]
    values = params_ref.shape[1]
    splats = params_ref.shape[2]
    table[...] = jnp.zeros(table.shape, F32)
    for turn in range(groups):
        for owner in range(owners):
            for camera in range(cameras):
                for place in range(cap):
                    block = send_ref[turn, camera, owner, place]
                    first = (camera * cap + place) * PROJ
                    into = (turn * cameras + camera) * 16
                    table[block, into : into + PROJ, :] += back_ref[
                        turn, owner, first : first + PROJ, :
                    ]
    matrix_high, matrix_low = split2(matrix_ref[...])
    both = jnp.concatenate([matrix_high, matrix_low], axis=1)
    for turn in range(groups):
        base = lax.rem(me + turn, groups) * share

        def block_step(place, _, turn=turn, base=base):
            block = base + place
            high, low = split2(table[block])
            gradient = dot32(both, jnp.concatenate([high, high], axis=0)) + dot32(matrix_high, low)
            gradient = gradient[:values]
            new_first = BETA_FIRST * firsts[turn][place] + (1.0 - BETA_FIRST) * gradient
            new_second = (
                BETA_SECOND * seconds[turn][place] + (1.0 - BETA_SECOND) * gradient * gradient
            )
            params_out[block] = params_ref[block] - RATE * new_first / (
                jnp.sqrt(new_second) + EPSILON
            )
            if turn == 0:
                first_out[place] = new_first
                second_out[place] = new_second
            return 0

        lax.fori_loop(0, share, block_step, 0, unroll=2)
    for owner in range(split_ref.shape[1]):
        alive = live_ref[0, owner].astype(F32)
        parent_out[owner, 0:values, :] = params_out[split_ref[0, owner]] * alive
        parent_out[owner, values : values + 1, :] = jnp.zeros((1, splats), F32) + alive


def update(send, split_block, split_live, back, matrix, params, firsts, seconds):
    groups = len(firsts)
    owned, values, splats = params.shape
    share = firsts[0].shape
    return pl.pallas_call(
        functools.partial(update_kernel, groups),
        out_shape=(
            jax.ShapeDtypeStruct(params.shape, F32),
            jax.ShapeDtypeStruct(share, F32),
            jax.ShapeDtypeStruct(share, F32),
            jax.ShapeDtypeStruct((split_block.shape[1], values + 1, splats), F32),
        ),
        in_specs=[SMEM, SMEM, SMEM] + [VMEM] * (3 + 2 * groups),
        out_specs=(VMEM,) * 4,
        scratch_shapes=[pltpu.VMEM((owned, matrix.shape[1], splats), F32)],
        compiler_params=pltpu.CompilerParams(vmem_limit_bytes=BIG),
        name="update",
    )(send, split_block, split_live, back, matrix, params, *firsts, *seconds)


def body(
    params, moment_first, moment_second, cam_proj, send_block,
    tile_slot, tile_count, targets, split_block, split_live,
):
    groups = lax.axis_size("cam")
    owners = lax.axis_size("dev")
    cameras, rows, values = cam_proj.shape
    cap = send_block.shape[3]
    splats = params.shape[2]
    padded = jnp.pad(cam_proj, ((0, 0), (0, 16 - rows), (0, 0)))
    outgoing = pl.pallas_call(
        project_kernel,
        out_shape=jax.ShapeDtypeStruct((owners, cameras * cap * PROJ, splats), F32),
        in_specs=[SMEM, VMEM, VMEM],
        out_specs=VMEM,
        scratch_shapes=[pltpu.VMEM((params.shape[0], cameras * 16, splats), F32)],
        compiler_params=pltpu.CompilerParams(vmem_limit_bytes=BIG),
        name="project",
    )(send_block, padded.reshape(cameras * 16, values), params)

    small = jnp.concatenate([padded.reshape(-1), send_block.astype(F32).reshape(-1)])
    smalls = [small]
    firsts = [moment_first[0, 0]]
    seconds = [moment_second[0, 0]]
    for turn in range(1, groups):
        pattern = [((one + turn) % groups, one) for one in range(groups)]
        smalls.append(lax.ppermute(small, "cam", pattern))
        firsts.append(lax.ppermute(moment_first[0, 0], "cam", pattern))
        seconds.append(lax.ppermute(moment_second[0, 0], "cam", pattern))
    joined = jnp.stack(smalls)
    sized = cameras * 16 * values
    matrix = joined[:, :sized].reshape(groups * cameras * 16, values).T
    matrix = jnp.pad(matrix, ((0, -values % 16), (0, 0)))
    sends = joined[:, sized:].astype(jnp.int32).reshape(groups, cameras, owners, cap)

    received = exchange(outgoing, "dev", 5)
    images, back = render(tile_slot, tile_count, received, targets)
    gathered = return_home(back, groups)
    new_params, new_first, new_second, parents = update(
        sends, split_block, split_live, gathered, matrix, params, firsts, seconds
    )
    arrived = exchange(parents, "dev", 6)
    alive = arrived[:, values:, :]
    parent = arrived[:, :values, :]
    offset = 0.5 * jnp.exp(parent[:, 3:6] - 1.0) * alive
    offset = jnp.pad(offset, ((0, 0), (0, values - 3), (0, 0)))
    line = lax.broadcasted_iota(jnp.int32, parent.shape, 1)
    shrunk = parent - jnp.where((line >= 3) & (line < 6), SHRINK, 0.0) * alive
    children = jnp.stack([shrunk + offset, shrunk - offset], axis=1)
    return (
        images,
        new_params,
        new_first.reshape(moment_first.shape),
        new_second.reshape(moment_second.shape),
        children,
    )


def solution(mesh):
    placed = (
        P("dev", None, None),
        P("dev", "cam", None, None, None),
        P("dev", "cam", None, None, None),
        P("cam", None, None),
        P("cam", "dev", None, None),
        P("cam", "dev", None),
        P("cam", "dev"),
        P("cam", "dev", None, None),
        P("dev", None),
        P("dev", None),
    )
    return jax.shard_map(
        body,
        mesh=mesh,
        in_specs=placed,
        out_specs=(
            P("cam", "dev", None, None),
            P("dev", None, None),
            P("dev", "cam", None, None, None),
            P("dev", "cam", None, None, None),
            P("dev", None, None, None),
        ),
        check_vma=False,
    )
```

```python
import functools
import math

import jax
import jax.numpy as jnp
from jax import lax
from jax.experimental import pallas as pl
from jax.experimental.pallas import tpu as pltpu
from jax.sharding import PartitionSpec as P

TSIDE = 16
PROJ = 9
LOSS_WEIGHT = 256.0
RATE = 0.01
BETA_FIRST = 0.9
BETA_SECOND = 0.999
EPSILON = 1e-08
SHRINK = math.log(1.6)
LOG2E = math.log2(math.e)
MESH = pl.DeviceIdType.MESH
HIGHEST = lax.Precision.HIGHEST
F32 = jnp.float32
BF16 = jnp.bfloat16
VMEM = pl.BlockSpec(memory_space=pltpu.VMEM)
SMEM = pl.BlockSpec(memory_space=pltpu.SMEM)
BIG = 60 * 1024 * 1024


def split2(value):
    high = value.astype(BF16)
    return high, (value - high.astype(F32)).astype(BF16)


def dot32(left, right, dims=(((1,), (0,)), ((), ()))):
    return lax.dot_general(left, right, dims, preferred_element_type=F32)


def softplus(value):
    return jnp.maximum(value, 0.0) + jnp.log(1.0 + jnp.exp(-jnp.abs(value)))


def sigmoid(value):
    return 1.0 / (1.0 + jnp.exp(-value))


def project_kernel(
    send_ref, matrix_ref, params_ref, out_ref, rows_ref, parcels, land, send_sems, recv_sems
):
    values, owned, _ = params_ref.shape
    cameras, _, owners, cap = send_ref.shape
    me = lax.axis_index("dev")
    barrier = pltpu.get_barrier_semaphore()
    for step in range(1, owners):
        pl.semaphore_signal(
            barrier, inc=1, device_id={"dev": lax.rem(me + step, owners)}, device_id_type=MESH
        )
    matrix = matrix_ref[:, :values]
    for block in range(owned):
        rows_ref[block] = jnp.dot(
            matrix, params_ref[:, block, :], precision=HIGHEST, preferred_element_type=F32
        )
    for owner in range(owners):
        for camera in range(cameras):
            for place in range(cap):
                chosen = send_ref[camera, 0, owner, place]
                first = (camera * cap + place) * PROJ
                parcels[owner, first : first + PROJ, :] = rows_ref[
                    chosen, camera * 16 : camera * 16 + PROJ, :
                ]
    pl.semaphore_wait(barrier, owners - 1)
    copies = []
    for step in range(1, owners):
        peer = lax.rem(me + step, owners)
        copy = pltpu.make_async_remote_copy(
            src_ref=parcels.at[peer],
            dst_ref=land.at[me],
            send_sem=send_sems.at[step - 1],
            recv_sem=recv_sems.at[step - 1],
            device_id={"dev": peer},
            device_id_type=MESH,
        )
        copy.start()
        copies.append(copy)
    out_ref[me] = parcels[me]
    for step in range(1, owners):
        copies[step - 1].wait_recv()
        source = lax.rem(me - step + owners, owners)
        out_ref[source] = land[source]
    for copy in copies:
        copy.wait_send()


def project(send_block, matrix, params):
    cameras, _, owners, cap = send_block.shape
    values, owned, splats = params.shape
    shape = (owners, cameras * cap * PROJ, splats)
    return pl.pallas_call(
        project_kernel,
        out_shape=jax.ShapeDtypeStruct(shape, F32),
        in_specs=[SMEM, VMEM, VMEM],
        out_specs=VMEM,
        scratch_shapes=[
            pltpu.VMEM((owned, matrix.shape[0], splats), F32),
            pltpu.VMEM(shape, F32),
            pltpu.VMEM(shape, F32),
            pltpu.SemaphoreType.DMA((owners - 1,)),
            pltpu.SemaphoreType.DMA((owners - 1,)),
        ],
        compiler_params=pltpu.CompilerParams(
            collective_id=5, has_side_effects=True, vmem_limit_bytes=BIG
        ),
        name="project",
    )(send_block, matrix, params)


def exchange_kernel(axis, count, x_ref, out_ref, land, send_sems, recv_sems):
    me = lax.axis_index(axis)
    barrier = pltpu.get_barrier_semaphore()
    for step in range(1, count):
        pl.semaphore_signal(
            barrier, inc=1, device_id={axis: lax.rem(me + step, count)}, device_id_type=MESH
        )
    pl.semaphore_wait(barrier, count - 1)
    copies = []
    for step in range(1, count):
        peer = lax.rem(me + step, count)
        copy = pltpu.make_async_remote_copy(
            src_ref=x_ref.at[peer],
            dst_ref=land.at[me],
            send_sem=send_sems.at[step - 1],
            recv_sem=recv_sems.at[step - 1],
            device_id={axis: peer},
            device_id_type=MESH,
        )
        copy.start()
        copies.append(copy)
    out_ref[me] = x_ref[me]
    for step in range(1, count):
        copies[step - 1].wait_recv()
        source = lax.rem(me - step + count, count)
        out_ref[source] = land[source]
    for copy in copies:
        copy.wait_send()


def exchange(x, axis, ident):
    count = x.shape[0]
    return pl.pallas_call(
        functools.partial(exchange_kernel, axis, count),
        out_shape=jax.ShapeDtypeStruct(x.shape, F32),
        in_specs=[VMEM],
        out_specs=VMEM,
        scratch_shapes=[
            pltpu.VMEM(x.shape, F32),
            pltpu.SemaphoreType.DMA((count - 1,)),
            pltpu.SemaphoreType.DMA((count - 1,)),
        ],
        compiler_params=pltpu.CompilerParams(
            collective_id=ident, has_side_effects=True, vmem_limit_bytes=BIG
        ),
        name=f"exchange_{ident}",
    )(x)


def return_kernel(owners, groups, x_ref, out_ref, land, zsend, zrecv, csend, crecv):
    me = lax.axis_index("dev")
    group = lax.axis_index("cam")
    barrier = pltpu.get_barrier_semaphore()
    for step in range(1, owners):
        pl.semaphore_signal(
            barrier, inc=1, device_id={"dev": lax.rem(me + step, owners)}, device_id_type=MESH
        )
    for step in range(1, groups):
        pl.semaphore_signal(
            barrier, inc=1, device_id={"cam": lax.rem(group + step, groups)}, device_id_type=MESH
        )
    pl.semaphore_wait(barrier, owners + groups - 2)
    along = []
    for step in range(1, owners):
        peer = lax.rem(me + step, owners)
        copy = pltpu.make_async_remote_copy(
            src_ref=x_ref.at[peer],
            dst_ref=land.at[0, me],
            send_sem=zsend.at[step - 1],
            recv_sem=zrecv.at[step - 1],
            device_id={"dev": peer},
            device_id_type=MESH,
        )
        copy.start()
        along.append(copy)
    across = []
    for step in range(owners):
        source = lax.rem(me - step + owners, owners)
        if step:
            along[step - 1].wait_recv()
        piece = land.at[0, source] if step else x_ref.at[me]
        for turn in range(1, groups):
            copy = pltpu.make_async_remote_copy(
                src_ref=piece,
                dst_ref=land.at[turn, source],
                send_sem=csend.at[turn - 1, step],
                recv_sem=crecv.at[turn - 1, step],
                device_id={"cam": lax.rem(group - turn + groups, groups)},
                device_id_type=MESH,
            )
            copy.start()
            across.append((turn, source, copy))
        out_ref[0, source] = land[0, source] if step else x_ref[me]
    for turn, source, copy in across:
        copy.wait_recv()
        out_ref[turn, source] = land[turn, source]
    for copy in along:
        copy.wait_send()
    for _, _, copy in across:
        copy.wait_send()


def return_home(x, groups):
    owners = x.shape[0]
    shape = (groups,) + x.shape
    return pl.pallas_call(
        functools.partial(return_kernel, owners, groups),
        out_shape=jax.ShapeDtypeStruct(shape, F32),
        in_specs=[VMEM],
        out_specs=VMEM,
        scratch_shapes=[
            pltpu.VMEM(shape, F32),
            pltpu.SemaphoreType.DMA((owners - 1,)),
            pltpu.SemaphoreType.DMA((owners - 1,)),
            pltpu.SemaphoreType.DMA((groups - 1, owners)),
            pltpu.SemaphoreType.DMA((groups - 1, owners)),
        ],
        compiler_params=pltpu.CompilerParams(
            collective_id=7, has_side_effects=True, vmem_limit_bytes=BIG
        ),
        name="return_home",
    )(x)


def shape_of(raw):
    turn_x = jnp.tanh(raw[0])
    turn_y = jnp.tanh(raw[1])
    conic_a = 0.02 + 0.1 * softplus(raw[2])
    conic_c = 0.02 + 0.1 * softplus(raw[4])
    turn_b = jnp.tanh(raw[3])
    root = jnp.sqrt(conic_a * conic_c)
    return turn_x, turn_y, conic_a, conic_c, turn_b, root


def render_kernel(
    slot_ref, count_ref, received_ref, target_ref, image_ref, back_ref,
    feats, grads, weights, pairs, ratios, carry, before, after_tri, cot_rows, cot_cols, picture,
):
    cameras, tiles, _ = slot_ref.shape
    owners, rows, splats = received_ref.shape
    cap = rows // (PROJ * cameras)
    centre = 0.5 * TSIDE
    spread = 0.375 * TSIDE
    pixels = TSIDE * TSIDE
    half = 128
    per_chunk = half // TSIDE

    feats[...] = jnp.zeros(feats.shape, F32)
    grads[...] = jnp.zeros(grads.shape, F32)
    for index in range(cameras * cap):
        raw = [received_ref[:, index * PROJ + k, :] for k in range(PROJ)]
        turn_x, turn_y, conic_a, conic_c, turn_b, root = shape_of(raw)
        conic_b = 0.9 * root * turn_b
        feats[:, index, 0, :] = centre + spread * turn_x
        feats[:, index, 1, :] = centre + spread * turn_y
        feats[:, index, 2, :] = (0.5 * LOG2E) * conic_a
        feats[:, index, 3, :] = LOG2E * conic_b
        feats[:, index, 4, :] = (0.5 * LOG2E) * conic_c
        feats[:, index, 5, :] = math.log2(0.99) - LOG2E * softplus(6.0 - raw[5])
        for k in range(3):
            feats[:, index, 8 + k, :] = sigmoid(raw[6 + k])

    row = lax.broadcasted_iota(jnp.int32, (splats, splats), 0)
    column = lax.broadcasted_iota(jnp.int32, (splats, splats), 1)
    ones = jnp.ones((splats, splats), BF16)
    lower = jnp.where(row < column, 1.0, 0.0).astype(BF16)
    upper = jnp.where(row > column, 1.0, 0.0).astype(BF16)
    for part in range(2):
        before[part * splats : (part + 1) * splats, :splats] = lower
        before[part * splats : (part + 1) * splats, splats:] = ones
        after_tri[part * splats : (part + 1) * splats, :splats] = upper
        after_tri[part * splats : (part + 1) * splats, splats:] = ones
    grid = lax.broadcasted_iota(jnp.int32, (TSIDE, splats), 0).astype(F32) + 0.5
    pad_rows = jnp.zeros((8, splats), F32)

    def entry_of(camera, tile, position):
        slot = slot_ref[camera, tile, position]
        return slot // cap, camera * cap + slot % cap

    def tile_step(number, _):
        camera = number // tiles
        tile = number % tiles
        live = count_ref[camera, tile]
        carry[...] = jnp.zeros(carry.shape, F32)
        picture[...] = jnp.zeros(picture.shape, F32)

        def forward(position, _):
            owner, index = entry_of(camera, tile, position)
            part = lambda k: feats[owner, index, k : k + 1, :]
            off_x = grid - part(0)
            off_y = grid - part(1)
            in_x = -(part(2) * off_x * off_x)
            cross = -(part(3) * off_x)
            in_y = part(5) - part(4) * off_y * off_y
            for chunk in range(pixels // half):
                where = slice(chunk * half, (chunk + 1) * half)
                lines = []
                for line in range(chunk * per_chunk, (chunk + 1) * per_chunk):
                    lines.append(in_x + (in_y[line : line + 1] + cross * off_y[line : line + 1]))
                alpha = jnp.exp2(jnp.concatenate(lines, axis=0))
                log_keep = jnp.log2(1.0 - alpha)
                summed = dot32(jnp.concatenate(split2(log_keep), axis=1), before[...])
                held = carry[where, :]
                weight = alpha * jnp.exp2(summed[:, :splats] + held)
                carry[where, :] = held + summed[:, splats:]
                weights[position, where, :] = weight
                pairs[position, where, :] = jnp.concatenate(split2(weight), axis=1)
                ratios[position, where, :] = alpha * jnp.exp2(-log_keep)
            colour_high, colour_low = split2(feats[owner, index, 8:16, :])
            colour_high = colour_high.astype(F32)
            colour_low = colour_low.astype(F32)
            shades = jnp.concatenate(
                [
                    jnp.concatenate([colour_high, colour_low], axis=0),
                    jnp.concatenate([colour_high, pad_rows], axis=0),
                ],
                axis=1,
            ).astype(BF16)
            drawn = dot32(shades, pairs[position], (((1,), (1,)), ((), ())))
            picture[...] += drawn[:8] + drawn[8:]
            return 0

        lax.fori_loop(0, live, forward, 0)
        for k in range(3):
            colour = picture[k : k + 1, :]
            image_ref[camera, k, pl.ds(tile, 1), :] = colour
            picture[k : k + 1, :] = LOSS_WEIGHT * (
                colour - target_ref[camera, k, pl.ds(tile, 1), :]
            )
        cot_high, cot_low = split2(picture[...])
        cot_high = cot_high.astype(F32)
        cot_low = cot_low.astype(F32)
        cot_rows[...] = jnp.concatenate([cot_high, cot_low], axis=0).astype(BF16)
        stacked = jnp.concatenate(
            [cot_high, cot_low, cot_high, jnp.zeros((half - 24, pixels), F32)], axis=0
        )
        cot_cols[...] = stacked.T.astype(BF16)
        carry[...] = jnp.zeros(carry.shape, F32)

        def backward(reverse, _):
            position = live - 1 - reverse
            owner, index = entry_of(camera, tile, position)
            part = lambda k: feats[owner, index, k : k + 1, :]
            off_x = grid - part(0)
            off_y = grid - part(1)
            colour_high, colour_low = split2(feats[owner, index, 8:16, :])
            colour_high = colour_high.astype(F32)
            shades = jnp.concatenate(
                [colour_high, colour_high, colour_low.astype(F32), jnp.zeros((half - 24, splats), F32)],
                axis=0,
            ).astype(BF16)
            total0 = jnp.zeros((TSIDE, splats), F32)
            total1 = jnp.zeros((TSIDE, splats), F32)
            total2 = jnp.zeros((TSIDE, splats), F32)
            for chunk in range(pixels // half):
                where = slice(chunk * half, (chunk + 1) * half)
                shade = dot32(cot_cols[where, :], shades)
                shaded = shade * weights[position, where, :]
                summed = dot32(jnp.concatenate(split2(shaded), axis=1), after_tri[...])
                held = carry[where, :]
                carry[where, :] = held + summed[:, splats:]
                pull = shaded - (summed[:, :splats] + held) * ratios[position, where, :]
                for line in range(per_chunk):
                    height = off_y[chunk * per_chunk + line : chunk * per_chunk + line + 1]
                    piece = pull[line * TSIDE : (line + 1) * TSIDE]
                    lifted = piece * height
                    total0 += piece
                    total1 += lifted
                    total2 += lifted * height
            sum_of = lambda value: jnp.sum(value, axis=0, keepdims=True)
            wide = total0 * off_x
            moments = jnp.concatenate(
                [
                    sum_of(total0),
                    sum_of(wide),
                    sum_of(total1),
                    sum_of(wide * off_x),
                    sum_of(total1 * off_x),
                    sum_of(total2),
                    jnp.zeros((2, splats), F32),
                ],
                axis=0,
            )
            tinted = dot32(cot_rows[...], pairs[position])
            grads[owner, index, 0:8, :] += moments
            grads[owner, index, 8:16, :] += (
                tinted[:8, :splats] + tinted[8:, :splats] + tinted[:8, splats:]
            )
            return 0

        lax.fori_loop(0, live, backward, 0)
        return 0

    lax.fori_loop(0, cameras * tiles, tile_step, 0)

    for index in range(cameras * cap):
        raw = [received_ref[:, index * PROJ + k, :] for k in range(PROJ)]
        turn_x, turn_y, conic_a, conic_c, turn_b, root = shape_of(raw)
        conic_b = 0.9 * root * turn_b
        sum0, sum_x, sum_y, sum_xx, sum_xy, sum_yy = [grads[:, index, k, :] for k in range(6)]
        grad_b = -sum_xy
        grad_a = -0.5 * sum_xx + grad_b * (0.5 * conic_b / conic_a)
        grad_c = -0.5 * sum_yy + grad_b * (0.5 * conic_b / conic_c)
        results = [
            (conic_a * sum_x + conic_b * sum_y) * (spread * (1.0 - turn_x * turn_x)),
            (conic_b * sum_x + conic_c * sum_y) * (spread * (1.0 - turn_y * turn_y)),
            grad_a * (0.1 * sigmoid(raw[2])),
            grad_b * (0.9 * root * (1.0 - turn_b * turn_b)),
            grad_c * (0.1 * sigmoid(raw[4])),
            sum0 * sigmoid(6.0 - raw[5]),
        ]
        for k in range(3):
            tone = sigmoid(raw[6 + k])
            results.append(grads[:, index, 8 + k, :] * (tone * (1.0 - tone)))
        for k in range(PROJ):
            back_ref[:, index * PROJ + k, :] = results[k]


def render(slots, counts, received, targets):
    owners, rows, splats = received.shape
    cameras, tiles, depth = slots.shape
    pixels = targets.shape[-1]
    cap = rows // (PROJ * cameras)
    return pl.pallas_call(
        render_kernel,
        out_shape=(
            jax.ShapeDtypeStruct(targets.shape, F32),
            jax.ShapeDtypeStruct(received.shape, F32),
        ),
        in_specs=[SMEM, SMEM, VMEM, VMEM],
        out_specs=(VMEM, VMEM),
        scratch_shapes=[
            pltpu.VMEM((owners, cameras * cap, 16, splats), F32),
            pltpu.VMEM((owners, cameras * cap, 16, splats), F32),
            pltpu.VMEM((depth, pixels, splats), F32),
            pltpu.VMEM((depth, pixels, 2 * splats), BF16),
            pltpu.VMEM((depth, pixels, splats), F32),
            pltpu.VMEM((pixels, splats), F32),
            pltpu.VMEM((2 * splats, 2 * splats), BF16),
            pltpu.VMEM((2 * splats, 2 * splats), BF16),
            pltpu.VMEM((16, pixels), BF16),
            pltpu.VMEM((pixels, 128), BF16),
            pltpu.VMEM((8, pixels), F32),
        ],
        compiler_params=pltpu.CompilerParams(vmem_limit_bytes=BIG),
        cost_estimate=pl.CostEstimate(
            flops=20_000_000_000, bytes_accessed=100_000_000, transcendentals=4_000_000
        ),
        name="render",
    )(slots, counts, received, targets)


def update_kernel(groups, *refs):
    send_ref, split_ref, live_ref, back_ref, params_ref = refs[:5]
    packs = refs[5 : 5 + groups]
    params_out, first_out, second_out, parent_out, table, slopes = refs[5 + groups :]
    me = lax.axis_index("cam")
    owners, rows = back_ref.shape[1:3]
    values, share, splats = first_out.shape
    cameras = table.shape[1] // (16 * groups)
    cap = rows // (PROJ * cameras)
    table[...] = jnp.zeros(table.shape, F32)
    for turn in range(groups):
        for owner in range(owners):
            for camera in range(cameras):
                for place in range(cap):
                    block = send_ref[turn, (camera * owners + owner) * cap + place]
                    first = (camera * cap + place) * PROJ
                    into = (turn * cameras + camera) * 16
                    table[block, into : into + PROJ, :] += back_ref[
                        turn, owner, first : first + PROJ, :
                    ]
    held = values * share
    stacked = jnp.concatenate(
        [pack[2 * held : 2 * held + 16 * cameras, :] for pack in packs], axis=0
    )
    matrix_high, matrix_low = split2(stacked.T[: -(-values // 16) * 16])
    both = jnp.concatenate([matrix_high, matrix_low], axis=1)
    for turn in range(groups):
        base = pl.multiple_of(lax.rem(me + turn, groups) * share, share)
        for place in range(share):
            high, low = split2(table[base + place])
            gradient = dot32(both, jnp.concatenate([high, high], axis=0)) + dot32(matrix_high, low)
            slopes[:, place, :] = gradient[:values]
        pack = packs[turn]
        for start in range(0, values, 8):
            end = min(values, start + 8)
            size = (end - start, share, splats)
            gradient = slopes[start:end]
            first = pack[start * share : end * share, :].reshape(size)
            second = pack[held + start * share : held + end * share, :].reshape(size)
            new_first = BETA_FIRST * first + (1.0 - BETA_FIRST) * gradient
            new_second = BETA_SECOND * second + (1.0 - BETA_SECOND) * gradient * gradient
            params_out[start:end, pl.ds(base, share), :] = params_ref[
                start:end, pl.ds(base, share), :
            ] - RATE * new_first / (jnp.sqrt(new_second) + EPSILON)
            if turn == 0:
                first_out[start:end] = new_first
                second_out[start:end] = new_second
    for owner in range(split_ref.shape[1]):
        alive = live_ref[0, owner].astype(F32)
        chosen = params_out[:, pl.ds(split_ref[0, owner], 1), :].reshape(values, splats)
        parent_out[owner, 0:values, :] = chosen * alive
        parent_out[owner, values : values + 1, :] = jnp.zeros((1, splats), F32) + alive


def update(sends, split_block, split_live, back, params, packs, share, cameras):
    groups = len(packs)
    values, owned, splats = params.shape
    moments = jax.ShapeDtypeStruct((values, share, splats), F32)
    return pl.pallas_call(
        functools.partial(update_kernel, groups),
        out_shape=(
            jax.ShapeDtypeStruct(params.shape, F32),
            moments,
            moments,
            jax.ShapeDtypeStruct((split_block.shape[1], values + 1, splats), F32),
        ),
        in_specs=[SMEM, SMEM, SMEM] + [VMEM] * (2 + groups),
        out_specs=(VMEM,) * 4,
        scratch_shapes=[
            pltpu.VMEM((owned, groups * 16 * cameras, splats), F32),
            pltpu.VMEM((values, share, splats), F32),
        ],
        compiler_params=pltpu.CompilerParams(vmem_limit_bytes=BIG),
        name="update",
    )(sends, split_block, split_live, back, params, *packs)


def divide_kernel(parent_ref, child_ref):
    values = parent_ref.shape[1] - 1
    line = lax.broadcasted_iota(jnp.int32, (values, parent_ref.shape[2]), 0)
    for owner in range(parent_ref.shape[0]):
        alive = parent_ref[owner, values : values + 1, :]
        parent = parent_ref[owner, 0:values, :]
        shift = jnp.concatenate(
            [
                0.5 * jnp.exp(parent[3:6] - 1.0) * alive,
                jnp.zeros((values - 3, parent.shape[1]), F32),
            ],
            axis=0,
        )
        shrunk = parent - jnp.where((line >= 3) & (line < 6), SHRINK, 0.0) * alive
        child_ref[owner, :, 0, :] = shrunk + shift
        child_ref[owner, :, 1, :] = shrunk - shift


def divide(parents):
    owners, rows, splats = parents.shape
    return pl.pallas_call(
        divide_kernel,
        out_shape=jax.ShapeDtypeStruct((owners, rows - 1, 2, splats), F32),
        in_specs=[VMEM],
        out_specs=VMEM,
        compiler_params=pltpu.CompilerParams(vmem_limit_bytes=BIG),
        name="divide",
    )(parents)


def body(
    params, moment_first, moment_second, cam_proj, send_block,
    tile_slot, tile_count, targets, split_block, split_live,
):
    groups = lax.axis_size("cam")
    cameras, rows, values = cam_proj.shape
    owned, _, splats = params.shape
    share = moment_first.shape[2]
    matrix = jnp.pad(cam_proj, ((0, 0), (0, 16 - rows), (0, 128 - values)))
    matrix = matrix.reshape(cameras * 16, 128)
    numbers = send_block.astype(F32).reshape(-1)
    numbers = jnp.pad(numbers, (0, -numbers.size % 1024)).reshape(-1, 128)
    by_value = lambda moment: moment[0, 0].transpose(1, 0, 2).reshape(values * share, splats)
    pack = jnp.concatenate([by_value(moment_first), by_value(moment_second), matrix, numbers])
    packs = [pack]
    for turn in range(1, groups):
        pattern = [((one + turn) % groups, one) for one in range(groups)]
        packs.append(lax.ppermute(pack, "cam", pattern))
    first_number = 2 * values * share + cameras * 16
    used = -(-send_block.size // 128)
    sends = jnp.stack([one[first_number : first_number + used].reshape(-1) for one in packs])
    sends = sends.astype(jnp.int32)

    by_block = params.transpose(1, 0, 2)
    received = project(send_block, matrix, by_block)
    images, back = render(tile_slot, tile_count, received, targets.transpose(0, 2, 1, 3))
    gathered = return_home(back, groups)
    new_params, new_first, new_second, parents = update(
        sends, split_block, split_live, gathered, by_block, packs, share, cameras
    )
    children = divide(exchange(parents, "dev", 6))
    restore = lambda moment: moment.transpose(1, 0, 2).reshape(moment_first.shape)
    return (
        images.transpose(0, 2, 1, 3),
        new_params.transpose(1, 0, 2),
        restore(new_first),
        restore(new_second),
        children.transpose(0, 2, 1, 3),
    )


def solution(mesh):
    placed = (
        P("dev", None, None),
        P("dev", "cam", None, None, None),
        P("dev", "cam", None, None, None),
        P("cam", None, None),
        P("cam", "dev", None, None),
        P("cam", "dev", None),
        P("cam", "dev"),
        P("cam", "dev", None, None),
        P("dev", None),
        P("dev", None),
    )
    return jax.shard_map(
        body,
        mesh=mesh,
        in_specs=placed,
        out_specs=(
            P("cam", "dev", None, None),
            P("dev", None, None),
            P("dev", "cam", None, None, None),
            P("dev", "cam", None, None, None),
            P("dev", None, None, None),
        ),
        check_vma=False,
    )
```

```python
import functools
import math

import jax
import jax.numpy as jnp
from jax import lax
from jax.experimental import pallas as pl
from jax.experimental.pallas import tpu as pltpu
from jax.sharding import PartitionSpec as P

TSIDE = 16
PROJ = 9
PAIR = 2
LOSS_WEIGHT = 256.0
RATE = 0.01
BETA_FIRST = 0.9
BETA_SECOND = 0.999
EPSILON = 1e-08
SHRINK = math.log(1.6)
LOG2E = math.log2(math.e)
MESH = pl.DeviceIdType.MESH
HIGHEST = lax.Precision.HIGHEST
F32 = jnp.float32
BF16 = jnp.bfloat16
VMEM = pl.BlockSpec(memory_space=pltpu.VMEM)
SMEM = pl.BlockSpec(memory_space=pltpu.SMEM)
BIG = 60 * 1024 * 1024


def split2(value):
    high = value.astype(BF16)
    return high, (value - high.astype(F32)).astype(BF16)


def dot32(left, right, dims=(((1,), (0,)), ((), ()))):
    return lax.dot_general(left, right, dims, preferred_element_type=F32)


def softplus(value):
    return jnp.maximum(value, 0.0) + jnp.log(1.0 + jnp.exp(-jnp.abs(value)))


def sigmoid(value):
    return 1.0 / (1.0 + jnp.exp(-value))


def project_kernel(
    send_ref, matrix_ref, params_ref, out_ref, rows_ref, parcels, land, send_sems, recv_sems
):
    values, owned, _ = params_ref.shape
    cameras, _, cap, owners = send_ref.shape
    me = lax.axis_index("dev")
    barrier = pltpu.get_barrier_semaphore()
    for step in range(1, owners):
        pl.semaphore_signal(
            barrier, inc=1, device_id={"dev": lax.rem(me + step, owners)}, device_id_type=MESH
        )
    matrix = matrix_ref[:, :values]
    for block in range(owned):
        rows_ref[block] = jnp.dot(
            matrix, params_ref[:, block, :], precision=HIGHEST, preferred_element_type=F32
        )
    for owner in range(owners):
        for camera in range(cameras):
            for place in range(cap):
                chosen = send_ref[camera, 0, place, owner]
                first = (camera * cap + place) * PROJ
                parcels[owner, first : first + PROJ, :] = rows_ref[
                    chosen, camera * 16 : camera * 16 + PROJ, :
                ]
    pl.semaphore_wait(barrier, owners - 1)
    copies = []
    for step in range(1, owners):
        peer = lax.rem(me + step, owners)
        copy = pltpu.make_async_remote_copy(
            src_ref=parcels.at[peer],
            dst_ref=land.at[me],
            send_sem=send_sems.at[step - 1],
            recv_sem=recv_sems.at[step - 1],
            device_id={"dev": peer},
            device_id_type=MESH,
        )
        copy.start()
        copies.append(copy)
    out_ref[me] = parcels[me]
    for step in range(1, owners):
        copies[step - 1].wait_recv()
        source = lax.rem(me - step + owners, owners)
        out_ref[source] = land[source]
    for copy in copies:
        copy.wait_send()


def project(send_block, matrix, params):
    cameras, _, cap, owners = send_block.shape
    values, owned, splats = params.shape
    shape = (owners, cameras * cap * PROJ, splats)
    return pl.pallas_call(
        project_kernel,
        out_shape=jax.ShapeDtypeStruct(shape, F32),
        in_specs=[SMEM, VMEM, VMEM],
        out_specs=VMEM,
        scratch_shapes=[
            pltpu.VMEM((owned, matrix.shape[0], splats), F32),
            pltpu.VMEM(shape, F32),
            pltpu.VMEM(shape, F32),
            pltpu.SemaphoreType.DMA((owners - 1,)),
            pltpu.SemaphoreType.DMA((owners - 1,)),
        ],
        compiler_params=pltpu.CompilerParams(
            collective_id=5, has_side_effects=True, vmem_limit_bytes=BIG
        ),
        name="project",
    )(send_block, matrix, params)


def exchange_kernel(axis, count, x_ref, out_ref, land, send_sems, recv_sems):
    me = lax.axis_index(axis)
    barrier = pltpu.get_barrier_semaphore()
    for step in range(1, count):
        pl.semaphore_signal(
            barrier, inc=1, device_id={axis: lax.rem(me + step, count)}, device_id_type=MESH
        )
    pl.semaphore_wait(barrier, count - 1)
    copies = []
    for step in range(1, count):
        peer = lax.rem(me + step, count)
        copy = pltpu.make_async_remote_copy(
            src_ref=x_ref.at[peer],
            dst_ref=land.at[me],
            send_sem=send_sems.at[step - 1],
            recv_sem=recv_sems.at[step - 1],
            device_id={axis: peer},
            device_id_type=MESH,
        )
        copy.start()
        copies.append(copy)
    out_ref[me] = x_ref[me]
    for step in range(1, count):
        copies[step - 1].wait_recv()
        source = lax.rem(me - step + count, count)
        out_ref[source] = land[source]
    for copy in copies:
        copy.wait_send()


def exchange(x, axis, ident):
    count = x.shape[0]
    return pl.pallas_call(
        functools.partial(exchange_kernel, axis, count),
        out_shape=jax.ShapeDtypeStruct(x.shape, F32),
        in_specs=[VMEM],
        out_specs=VMEM,
        scratch_shapes=[
            pltpu.VMEM(x.shape, F32),
            pltpu.SemaphoreType.DMA((count - 1,)),
            pltpu.SemaphoreType.DMA((count - 1,)),
        ],
        compiler_params=pltpu.CompilerParams(
            collective_id=ident, has_side_effects=True, vmem_limit_bytes=BIG
        ),
        name=f"exchange_{ident}",
    )(x)


def return_kernel(owners, groups, x_ref, out_ref, land, zsend, zrecv, csend, crecv):
    me = lax.axis_index("dev")
    group = lax.axis_index("cam")
    barrier = pltpu.get_barrier_semaphore()
    for step in range(1, owners):
        pl.semaphore_signal(
            barrier, inc=1, device_id={"dev": lax.rem(me + step, owners)}, device_id_type=MESH
        )
    for step in range(1, groups):
        pl.semaphore_signal(
            barrier, inc=1, device_id={"cam": lax.rem(group + step, groups)}, device_id_type=MESH
        )
    pl.semaphore_wait(barrier, owners + groups - 2)
    along = []
    for step in range(1, owners):
        peer = lax.rem(me + step, owners)
        copy = pltpu.make_async_remote_copy(
            src_ref=x_ref.at[peer],
            dst_ref=land.at[0, me],
            send_sem=zsend.at[step - 1],
            recv_sem=zrecv.at[step - 1],
            device_id={"dev": peer},
            device_id_type=MESH,
        )
        copy.start()
        along.append(copy)
    across = []
    for step in range(owners):
        source = lax.rem(me - step + owners, owners)
        if step:
            along[step - 1].wait_recv()
        piece = land.at[0, source] if step else x_ref.at[me]
        for turn in range(1, groups):
            copy = pltpu.make_async_remote_copy(
                src_ref=piece,
                dst_ref=land.at[turn, source],
                send_sem=csend.at[turn - 1, step],
                recv_sem=crecv.at[turn - 1, step],
                device_id={"cam": lax.rem(group - turn + groups, groups)},
                device_id_type=MESH,
            )
            copy.start()
            across.append((turn, source, copy))
        out_ref[0, source] = land[0, source] if step else x_ref[me]
    for turn, source, copy in across:
        copy.wait_recv()
        out_ref[turn, source] = land[turn, source]
    for copy in along:
        copy.wait_send()
    for _, _, copy in across:
        copy.wait_send()


def return_home(x, groups):
    owners = x.shape[0]
    shape = (groups,) + x.shape
    return pl.pallas_call(
        functools.partial(return_kernel, owners, groups),
        out_shape=jax.ShapeDtypeStruct(shape, F32),
        in_specs=[VMEM],
        out_specs=VMEM,
        scratch_shapes=[
            pltpu.VMEM(shape, F32),
            pltpu.SemaphoreType.DMA((owners - 1,)),
            pltpu.SemaphoreType.DMA((owners - 1,)),
            pltpu.SemaphoreType.DMA((groups - 1, owners)),
            pltpu.SemaphoreType.DMA((groups - 1, owners)),
        ],
        compiler_params=pltpu.CompilerParams(
            collective_id=7, has_side_effects=True, vmem_limit_bytes=BIG
        ),
        name="return_home",
    )(x)


def shape_of(raw):
    turn_x = jnp.tanh(raw[0])
    turn_y = jnp.tanh(raw[1])
    conic_a = 0.02 + 0.1 * softplus(raw[2])
    conic_c = 0.02 + 0.1 * softplus(raw[4])
    turn_b = jnp.tanh(raw[3])
    root = jnp.sqrt(conic_a * conic_c)
    return turn_x, turn_y, conic_a, conic_c, turn_b, root


def render_kernel(
    slot_ref, count_ref, received_ref, target_ref, image_ref, back_ref,
    feats, grads, weights, pairs, ratios, carry, before, after_tri, cot_rows, cot_cols, picture,
):
    cameras, tiles, _ = slot_ref.shape
    owners, rows, splats = received_ref.shape
    cap = rows // (PROJ * cameras)
    centre = 0.5 * TSIDE
    spread = 0.375 * TSIDE
    pixels = TSIDE * TSIDE
    half = 128
    per_chunk = half // TSIDE

    feats[...] = jnp.zeros(feats.shape, F32)
    grads[...] = jnp.zeros(grads.shape, F32)
    for index in range(cameras * cap):
        raw = [received_ref[:, index * PROJ + k, :] for k in range(PROJ)]
        turn_x, turn_y, conic_a, conic_c, turn_b, root = shape_of(raw)
        conic_b = 0.9 * root * turn_b
        feats[:, index, 0, :] = centre + spread * turn_x
        feats[:, index, 1, :] = centre + spread * turn_y
        feats[:, index, 2, :] = (0.5 * LOG2E) * conic_a
        feats[:, index, 3, :] = LOG2E * conic_b
        feats[:, index, 4, :] = (0.5 * LOG2E) * conic_c
        feats[:, index, 5, :] = math.log2(0.99) - LOG2E * softplus(6.0 - raw[5])
        for k in range(3):
            feats[:, index, 8 + k, :] = sigmoid(raw[6 + k])

    row = lax.broadcasted_iota(jnp.int32, (splats, splats), 0)
    column = lax.broadcasted_iota(jnp.int32, (splats, splats), 1)
    ones = jnp.ones((splats, splats), BF16)
    lower = jnp.where(row < column, 1.0, 0.0).astype(BF16)
    upper = jnp.where(row > column, 1.0, 0.0).astype(BF16)
    for part in range(2):
        before[part * splats : (part + 1) * splats, :splats] = lower
        before[part * splats : (part + 1) * splats, splats:] = ones
        after_tri[part * splats : (part + 1) * splats, :splats] = upper
        after_tri[part * splats : (part + 1) * splats, splats:] = ones
    grid = lax.broadcasted_iota(jnp.int32, (TSIDE, splats), 0).astype(F32) + 0.5
    pad_rows = jnp.zeros((8, splats), F32)

    def entry_of(camera, tile, position):
        slot = slot_ref[camera, tile, position]
        return slot // cap, camera * cap + slot % cap

    def tile_step(number, _):
        camera = number // tiles
        tile = number % tiles
        live = count_ref[camera, tile]
        carry[...] = jnp.zeros(carry.shape, F32)
        picture[...] = jnp.zeros(picture.shape, F32)

        def forward(pair, _):
            places = [PAIR * pair + sub for sub in range(PAIR)]
            alphas, logs, sums, shades = [], [], [], []
            for place in places:
                owner, index = entry_of(camera, tile, jnp.minimum(place, live - 1))
                part = lambda k: feats[owner, index, k : k + 1, :]
                off_x = grid - part(0)
                off_y = grid - part(1)
                in_x = -(part(2) * off_x * off_x)
                cross = -(part(3) * off_x)
                faint = jnp.where(place < live, part(5), -1e30)
                in_y = faint - part(4) * off_y * off_y
                for chunk in range(pixels // half):
                    lines = []
                    for line in range(chunk * per_chunk, (chunk + 1) * per_chunk):
                        lines.append(
                            in_x + (in_y[line : line + 1] + cross * off_y[line : line + 1])
                        )
                    alpha = jnp.exp2(jnp.concatenate(lines, axis=0))
                    log_keep = jnp.log2(1.0 - alpha)
                    alphas.append(alpha)
                    logs.append(log_keep)
                    sums.append(dot32(jnp.concatenate(split2(log_keep), axis=1), before[...]))
                colour_high, colour_low = split2(feats[owner, index, 8:16, :])
                colour_high = colour_high.astype(F32)
                colour_low = colour_low.astype(F32)
                shades.append(
                    jnp.concatenate(
                        [
                            jnp.concatenate([colour_high, colour_low], axis=0),
                            jnp.concatenate([colour_high, pad_rows], axis=0),
                        ],
                        axis=1,
                    ).astype(BF16)
                )
            chunks = pixels // half
            for chunk in range(chunks):
                where = slice(chunk * half, (chunk + 1) * half)
                held = carry[where, :]
                drawn = jnp.zeros((16, half), F32)
                for sub, place in enumerate(places):
                    at = sub * chunks + chunk
                    weight = alphas[at] * jnp.exp2(sums[at][:, :splats] + held)
                    held = held + sums[at][:, splats:]
                    both = jnp.concatenate(split2(weight), axis=1)
                    weights[place, where, :] = weight
                    pairs[place, where, :] = both
                    ratios[place, where, :] = alphas[at] * jnp.exp2(-logs[at])
                    drawn += dot32(shades[sub], both, (((1,), (1,)), ((), ())))
                carry[where, :] = held
                picture[:, where] += drawn[:8] + drawn[8:]
            return 0

        steps = (live + PAIR - 1) // PAIR
        lax.fori_loop(0, steps, forward, 0)
        for k in range(3):
            colour = picture[k : k + 1, :]
            image_ref[camera, k, pl.ds(tile, 1), :] = colour
            picture[k : k + 1, :] = LOSS_WEIGHT * (
                colour - target_ref[camera, k, pl.ds(tile, 1), :]
            )
        cot_high, cot_low = split2(picture[...])
        cot_high = cot_high.astype(F32)
        cot_low = cot_low.astype(F32)
        cot_rows[...] = jnp.concatenate([cot_high, cot_low], axis=0).astype(BF16)
        stacked = jnp.concatenate(
            [cot_high, cot_low, cot_high, jnp.zeros((half - 24, pixels), F32)], axis=0
        )
        cot_cols[...] = stacked.T.astype(BF16)
        carry[...] = jnp.zeros(carry.shape, F32)

        def backward(reverse, _):
            places = [PAIR * (steps - 1 - reverse) + PAIR - 1 - sub for sub in range(PAIR)]
            chunks = pixels // half
            spots, offsets, shaded, sums = [], [], [], []
            for place in places:
                owner, index = entry_of(camera, tile, jnp.minimum(place, live - 1))
                spots.append((owner, index))
                offsets.append(
                    (grid - feats[owner, index, 0:1, :], grid - feats[owner, index, 1:2, :])
                )
                colour_high, colour_low = split2(feats[owner, index, 8:16, :])
                colour_high = colour_high.astype(F32)
                shades = jnp.concatenate(
                    [
                        colour_high,
                        colour_high,
                        colour_low.astype(F32),
                        jnp.zeros((half - 24, splats), F32),
                    ],
                    axis=0,
                ).astype(BF16)
                for chunk in range(chunks):
                    where = slice(chunk * half, (chunk + 1) * half)
                    piece = dot32(cot_cols[where, :], shades) * weights[place, where, :]
                    shaded.append(piece)
                    sums.append(dot32(jnp.concatenate(split2(piece), axis=1), after_tri[...]))
            totals = [[jnp.zeros((TSIDE, splats), F32)] * 3 for _ in places]
            for chunk in range(chunks):
                where = slice(chunk * half, (chunk + 1) * half)
                held = carry[where, :]
                for sub, place in enumerate(places):
                    at = sub * chunks + chunk
                    pull = shaded[at] - (sums[at][:, :splats] + held) * ratios[place, where, :]
                    held = held + sums[at][:, splats:]
                    total0, total1, total2 = totals[sub]
                    off_y = offsets[sub][1]
                    for line in range(per_chunk):
                        height = off_y[chunk * per_chunk + line : chunk * per_chunk + line + 1]
                        piece = pull[line * TSIDE : (line + 1) * TSIDE]
                        lifted = piece * height
                        total0 += piece
                        total1 += lifted
                        total2 += lifted * height
                    totals[sub] = [total0, total1, total2]
                carry[where, :] = held
            sum_of = lambda value: jnp.sum(value, axis=0, keepdims=True)
            for sub, place in enumerate(places):
                owner, index = spots[sub]
                total0, total1, total2 = totals[sub]
                off_x = offsets[sub][0]
                wide = total0 * off_x
                moments = jnp.concatenate(
                    [
                        sum_of(total0),
                        sum_of(wide),
                        sum_of(total1),
                        sum_of(wide * off_x),
                        sum_of(total1 * off_x),
                        sum_of(total2),
                        jnp.zeros((2, splats), F32),
                    ],
                    axis=0,
                )
                tinted = dot32(cot_rows[...], pairs[place])
                grads[owner, index, 0:8, :] += moments
                grads[owner, index, 8:16, :] += (
                    tinted[:8, :splats] + tinted[8:, :splats] + tinted[:8, splats:]
                )
            return 0

        lax.fori_loop(0, steps, backward, 0)
        return 0

    lax.fori_loop(0, cameras * tiles, tile_step, 0)

    for index in range(cameras * cap):
        raw = [received_ref[:, index * PROJ + k, :] for k in range(PROJ)]
        turn_x, turn_y, conic_a, conic_c, turn_b, root = shape_of(raw)
        conic_b = 0.9 * root * turn_b
        sum0, sum_x, sum_y, sum_xx, sum_xy, sum_yy = [grads[:, index, k, :] for k in range(6)]
        grad_b = -sum_xy
        grad_a = -0.5 * sum_xx + grad_b * (0.5 * conic_b / conic_a)
        grad_c = -0.5 * sum_yy + grad_b * (0.5 * conic_b / conic_c)
        results = [
            (conic_a * sum_x + conic_b * sum_y) * (spread * (1.0 - turn_x * turn_x)),
            (conic_b * sum_x + conic_c * sum_y) * (spread * (1.0 - turn_y * turn_y)),
            grad_a * (0.1 * sigmoid(raw[2])),
            grad_b * (0.9 * root * (1.0 - turn_b * turn_b)),
            grad_c * (0.1 * sigmoid(raw[4])),
            sum0 * sigmoid(6.0 - raw[5]),
        ]
        for k in range(3):
            tone = sigmoid(raw[6 + k])
            results.append(grads[:, index, 8 + k, :] * (tone * (1.0 - tone)))
        for k in range(PROJ):
            back_ref[:, index * PROJ + k, :] = results[k]


def render(slots, counts, received, targets):
    owners, rows, splats = received.shape
    cameras, tiles, depth = slots.shape
    pixels = targets.shape[-1]
    cap = rows // (PROJ * cameras)
    depth = -(-depth // PAIR) * PAIR
    return pl.pallas_call(
        render_kernel,
        out_shape=(
            jax.ShapeDtypeStruct(targets.shape, F32),
            jax.ShapeDtypeStruct(received.shape, F32),
        ),
        in_specs=[SMEM, SMEM, VMEM, VMEM],
        out_specs=(VMEM, VMEM),
        scratch_shapes=[
            pltpu.VMEM((owners, cameras * cap, 16, splats), F32),
            pltpu.VMEM((owners, cameras * cap, 16, splats), F32),
            pltpu.VMEM((depth, pixels, splats), F32),
            pltpu.VMEM((depth, pixels, 2 * splats), BF16),
            pltpu.VMEM((depth, pixels, splats), F32),
            pltpu.VMEM((pixels, splats), F32),
            pltpu.VMEM((2 * splats, 2 * splats), BF16),
            pltpu.VMEM((2 * splats, 2 * splats), BF16),
            pltpu.VMEM((16, pixels), BF16),
            pltpu.VMEM((pixels, 128), BF16),
            pltpu.VMEM((8, pixels), F32),
        ],
        compiler_params=pltpu.CompilerParams(vmem_limit_bytes=BIG),
        cost_estimate=pl.CostEstimate(
            flops=20_000_000_000, bytes_accessed=100_000_000, transcendentals=4_000_000
        ),
        name="render",
    )(slots, counts, received, targets)


def update_kernel(groups, *refs):
    send_ref, split_ref, live_ref, back_ref, params_hbm = refs[:5]
    packs_hbm = refs[5 : 5 + groups]
    (params_out, first_out, second_out, parent_out) = refs[5 + groups : 9 + groups]
    table, slopes, params_ref, packs, arrivals = refs[9 + groups :]
    loads = [
        pltpu.make_async_copy(packs_hbm[turn], packs.at[turn], arrivals.at[turn])
        for turn in range(groups)
    ]
    loads.append(pltpu.make_async_copy(params_hbm, params_ref, arrivals.at[groups]))
    for load in loads:
        load.start()
    me = lax.axis_index("cam")
    owners, rows = back_ref.shape[1:3]
    values, share, splats = first_out.shape
    cameras = table.shape[1] // (16 * groups)
    cap = rows // (PROJ * cameras)
    table[...] = jnp.zeros(table.shape, F32)
    for turn in range(groups):
        for owner in range(owners):
            for camera in range(cameras):
                for place in range(cap):
                    block = send_ref[turn, (camera * cap + place) * owners + owner]
                    first = (camera * cap + place) * PROJ
                    into = (turn * cameras + camera) * 16
                    table[block, into : into + PROJ, :] += back_ref[
                        turn, owner, first : first + PROJ, :
                    ]
    held = values * share
    for load in loads:
        load.wait()
    stacked = jnp.concatenate(
        [packs[turn, 2 * held : 2 * held + 16 * cameras, :] for turn in range(groups)], axis=0
    )
    matrix_high, matrix_low = split2(stacked.T[: -(-values // 16) * 16])
    both = jnp.concatenate([matrix_high, matrix_low], axis=1)
    for turn in range(groups):
        base = pl.multiple_of(lax.rem(me + turn, groups) * share, share)
        for place in range(share):
            high, low = split2(table[base + place])
            gradient = dot32(both, jnp.concatenate([high, high], axis=0)) + dot32(matrix_high, low)
            slopes[:, place, :] = gradient[:values]
        pack = packs.at[turn]
        for start in range(0, values, 8):
            end = min(values, start + 8)
            size = (end - start, share, splats)
            gradient = slopes[start:end]
            first = pack[start * share : end * share, :].reshape(size)
            second = pack[held + start * share : held + end * share, :].reshape(size)
            new_first = BETA_FIRST * first + (1.0 - BETA_FIRST) * gradient
            new_second = BETA_SECOND * second + (1.0 - BETA_SECOND) * gradient * gradient
            params_out[start:end, pl.ds(base, share), :] = params_ref[
                start:end, pl.ds(base, share), :
            ] - RATE * new_first / (jnp.sqrt(new_second) + EPSILON)
            if turn == 0:
                first_out[start:end] = new_first
                second_out[start:end] = new_second
    for owner in range(split_ref.shape[1]):
        alive = live_ref[0, owner].astype(F32)
        chosen = params_out[:, pl.ds(split_ref[0, owner], 1), :].reshape(values, splats)
        parent_out[owner, 0:values, :] = chosen * alive
        parent_out[owner, values : values + 1, :] = jnp.zeros((1, splats), F32) + alive


def update(sends, split_block, split_live, back, params, packs, share, cameras):
    groups = len(packs)
    values, owned, splats = params.shape
    moments = jax.ShapeDtypeStruct((values, share, splats), F32)
    return pl.pallas_call(
        functools.partial(update_kernel, groups),
        out_shape=(
            jax.ShapeDtypeStruct(params.shape, F32),
            moments,
            moments,
            jax.ShapeDtypeStruct((split_block.shape[1], values + 1, splats), F32),
        ),
        in_specs=[SMEM, SMEM, SMEM, VMEM] + [pl.BlockSpec(memory_space=pl.ANY)] * (1 + groups),
        out_specs=(VMEM,) * 4,
        scratch_shapes=[
            pltpu.VMEM((owned, groups * 16 * cameras, splats), F32),
            pltpu.VMEM((values, share, splats), F32),
            pltpu.VMEM(params.shape, F32),
            pltpu.VMEM((groups,) + packs[0].shape, F32),
            pltpu.SemaphoreType.DMA((groups + 1,)),
        ],
        compiler_params=pltpu.CompilerParams(vmem_limit_bytes=BIG),
        name="update",
    )(sends, split_block, split_live, back, params, *packs)


def divide_kernel(parent_ref, child_ref):
    values = parent_ref.shape[1] - 1
    line = lax.broadcasted_iota(jnp.int32, (values, parent_ref.shape[2]), 0)
    for owner in range(parent_ref.shape[0]):
        alive = parent_ref[owner, values : values + 1, :]
        parent = parent_ref[owner, 0:values, :]
        shift = jnp.concatenate(
            [
                0.5 * jnp.exp(parent[3:6] - 1.0) * alive,
                jnp.zeros((values - 3, parent.shape[1]), F32),
            ],
            axis=0,
        )
        shrunk = parent - jnp.where((line >= 3) & (line < 6), SHRINK, 0.0) * alive
        child_ref[owner, :, 0, :] = shrunk + shift
        child_ref[owner, :, 1, :] = shrunk - shift


def divide(parents):
    owners, rows, splats = parents.shape
    return pl.pallas_call(
        divide_kernel,
        out_shape=jax.ShapeDtypeStruct((owners, rows - 1, 2, splats), F32),
        in_specs=[VMEM],
        out_specs=VMEM,
        compiler_params=pltpu.CompilerParams(vmem_limit_bytes=BIG),
        name="divide",
    )(parents)


def body(
    params, moment_first, moment_second, cam_proj, send_block,
    tile_slot, tile_count, targets, split_block, split_live,
):
    groups = lax.axis_size("cam")
    cameras, rows, values = cam_proj.shape
    owned, _, splats = params.shape
    share = moment_first.shape[2]
    matrix = jnp.pad(cam_proj, ((0, 0), (0, 16 - rows), (0, 128 - values)))
    matrix = matrix.reshape(cameras * 16, 128)
    send_block = send_block.transpose(0, 1, 3, 2)
    numbers = send_block.astype(F32).reshape(-1)
    numbers = jnp.pad(numbers, (0, -numbers.size % 1024)).reshape(-1, 128)
    by_value = lambda moment: moment[0, 0].transpose(1, 0, 2).reshape(values * share, splats)
    pack = jnp.concatenate([by_value(moment_first), by_value(moment_second), matrix, numbers])
    packs = [pack]
    for turn in range(1, groups):
        pattern = [((one + turn) % groups, one) for one in range(groups)]
        packs.append(lax.ppermute(pack, "cam", pattern))
    first_number = 2 * values * share + cameras * 16
    used = -(-send_block.size // 128)
    sends = jnp.stack([one[first_number : first_number + used].reshape(-1) for one in packs])
    sends = sends.astype(jnp.int32)

    by_block = params.transpose(1, 0, 2)
    received = project(send_block, matrix, by_block)
    images, back = render(tile_slot, tile_count, received, targets.transpose(0, 2, 1, 3))
    gathered = return_home(back, groups)
    new_params, new_first, new_second, parents = update(
        sends, split_block, split_live, gathered, by_block, packs, share, cameras
    )
    children = divide(exchange(parents, "dev", 6))
    restore = lambda moment: moment.transpose(1, 0, 2).reshape(moment_first.shape)
    return (
        images.transpose(0, 2, 1, 3),
        new_params.transpose(1, 0, 2),
        restore(new_first),
        restore(new_second),
        children.transpose(0, 2, 1, 3),
    )


def solution(mesh):
    placed = (
        P("dev", None, None),
        P("dev", "cam", None, None, None),
        P("dev", "cam", None, None, None),
        P("cam", None, None),
        P("cam", "dev", None, None),
        P("cam", "dev", None),
        P("cam", "dev"),
        P("cam", "dev", None, None),
        P("dev", None),
        P("dev", None),
    )
    return jax.shard_map(
        body,
        mesh=mesh,
        in_specs=placed,
        out_specs=(
            P("cam", "dev", None, None),
            P("dev", None, None),
            P("dev", "cam", None, None, None),
            P("dev", "cam", None, None, None),
            P("dev", None, None, None),
        ),
        check_vma=False,
    )
```

```python
import functools
import math

import jax
import jax.numpy as jnp
from jax import lax
from jax.experimental import pallas as pl
from jax.experimental.pallas import tpu as pltpu
from jax.sharding import PartitionSpec as P

TSIDE = 16
PROJ = 9
PAIR = 2
LOSS_WEIGHT = 256.0
RATE = 0.01
BETA_FIRST = 0.9
BETA_SECOND = 0.999
EPSILON = 1e-08
SHRINK = math.log(1.6)
LOG2E = math.log2(math.e)
MESH = pl.DeviceIdType.MESH
HIGHEST = lax.Precision.HIGHEST
F32 = jnp.float32
BF16 = jnp.bfloat16
VMEM = pl.BlockSpec(memory_space=pltpu.VMEM)
SMEM = pl.BlockSpec(memory_space=pltpu.SMEM)
BIG = 60 * 1024 * 1024


def split2(value):
    high = value.astype(BF16)
    return high, (value - high.astype(F32)).astype(BF16)


def dot32(left, right, dims=(((1,), (0,)), ((), ()))):
    return lax.dot_general(left, right, dims, preferred_element_type=F32)


def softplus(value):
    return jnp.maximum(value, 0.0) + jnp.log(1.0 + jnp.exp(-jnp.abs(value)))


def sigmoid(value):
    return 1.0 / (1.0 + jnp.exp(-value))


def project_kernel(
    send_ref, matrix_ref, params_ref, out_ref, rows_ref, parcels, land, send_sems, recv_sems
):
    values, owned, _ = params_ref.shape
    cameras, _, cap, owners = send_ref.shape
    me = lax.axis_index("dev")
    barrier = pltpu.get_barrier_semaphore()
    for step in range(1, owners):
        pl.semaphore_signal(
            barrier, inc=1, device_id={"dev": lax.rem(me + step, owners)}, device_id_type=MESH
        )
    matrix_high, matrix_low = split2(matrix_ref[:, :values])
    both = jnp.concatenate([matrix_high, matrix_low], axis=0)
    lines = matrix_ref.shape[0]
    for block in range(owned):
        high, low = split2(params_ref[:, block, :])
        wide = dot32(both, high)
        rows_ref[block] = wide[:lines] + (wide[lines:] + dot32(matrix_high, low))
    for owner in range(owners):
        for camera in range(cameras):
            for place in range(cap):
                chosen = send_ref[camera, 0, place, owner]
                first = (camera * cap + place) * PROJ
                parcels[owner, first : first + PROJ, :] = rows_ref[
                    chosen, camera * 16 : camera * 16 + PROJ, :
                ]
    pl.semaphore_wait(barrier, owners - 1)
    copies = []
    for step in range(1, owners):
        peer = lax.rem(me + step, owners)
        copy = pltpu.make_async_remote_copy(
            src_ref=parcels.at[peer],
            dst_ref=land.at[me],
            send_sem=send_sems.at[step - 1],
            recv_sem=recv_sems.at[step - 1],
            device_id={"dev": peer},
            device_id_type=MESH,
        )
        copy.start()
        copies.append(copy)
    out_ref[me] = parcels[me]
    for step in range(1, owners):
        copies[step - 1].wait_recv()
        source = lax.rem(me - step + owners, owners)
        out_ref[source] = land[source]
    for copy in copies:
        copy.wait_send()


def project(send_block, matrix, params):
    cameras, _, cap, owners = send_block.shape
    values, owned, splats = params.shape
    shape = (owners, cameras * cap * PROJ, splats)
    return pl.pallas_call(
        project_kernel,
        out_shape=jax.ShapeDtypeStruct(shape, F32),
        in_specs=[SMEM, VMEM, VMEM],
        out_specs=VMEM,
        scratch_shapes=[
            pltpu.VMEM((owned, matrix.shape[0], splats), F32),
            pltpu.VMEM(shape, F32),
            pltpu.VMEM(shape, F32),
            pltpu.SemaphoreType.DMA((owners - 1,)),
            pltpu.SemaphoreType.DMA((owners - 1,)),
        ],
        compiler_params=pltpu.CompilerParams(
            collective_id=5, has_side_effects=True, vmem_limit_bytes=BIG
        ),
        name="project",
    )(send_block, matrix, params)


def exchange_kernel(axis, count, x_ref, out_ref, land, send_sems, recv_sems):
    me = lax.axis_index(axis)
    barrier = pltpu.get_barrier_semaphore()
    for step in range(1, count):
        pl.semaphore_signal(
            barrier, inc=1, device_id={axis: lax.rem(me + step, count)}, device_id_type=MESH
        )
    pl.semaphore_wait(barrier, count - 1)
    copies = []
    for step in range(1, count):
        peer = lax.rem(me + step, count)
        copy = pltpu.make_async_remote_copy(
            src_ref=x_ref.at[peer],
            dst_ref=land.at[me],
            send_sem=send_sems.at[step - 1],
            recv_sem=recv_sems.at[step - 1],
            device_id={axis: peer},
            device_id_type=MESH,
        )
        copy.start()
        copies.append(copy)
    out_ref[me] = x_ref[me]
    for step in range(1, count):
        copies[step - 1].wait_recv()
        source = lax.rem(me - step + count, count)
        out_ref[source] = land[source]
    for copy in copies:
        copy.wait_send()


def exchange(x, axis, ident):
    count = x.shape[0]
    return pl.pallas_call(
        functools.partial(exchange_kernel, axis, count),
        out_shape=jax.ShapeDtypeStruct(x.shape, F32),
        in_specs=[VMEM],
        out_specs=VMEM,
        scratch_shapes=[
            pltpu.VMEM(x.shape, F32),
            pltpu.SemaphoreType.DMA((count - 1,)),
            pltpu.SemaphoreType.DMA((count - 1,)),
        ],
        compiler_params=pltpu.CompilerParams(
            collective_id=ident, has_side_effects=True, vmem_limit_bytes=BIG
        ),
        name=f"exchange_{ident}",
    )(x)


def return_kernel(owners, groups, x_ref, out_ref, land, zsend, zrecv, csend, crecv):
    me = lax.axis_index("dev")
    group = lax.axis_index("cam")
    barrier = pltpu.get_barrier_semaphore()
    for step in range(1, owners):
        pl.semaphore_signal(
            barrier, inc=1, device_id={"dev": lax.rem(me + step, owners)}, device_id_type=MESH
        )
    for step in range(1, groups):
        pl.semaphore_signal(
            barrier, inc=1, device_id={"cam": lax.rem(group + step, groups)}, device_id_type=MESH
        )
    pl.semaphore_wait(barrier, owners + groups - 2)
    along = []
    for step in range(1, owners):
        peer = lax.rem(me + step, owners)
        copy = pltpu.make_async_remote_copy(
            src_ref=x_ref.at[peer],
            dst_ref=land.at[0, me],
            send_sem=zsend.at[step - 1],
            recv_sem=zrecv.at[step - 1],
            device_id={"dev": peer},
            device_id_type=MESH,
        )
        copy.start()
        along.append(copy)
    across = []
    for step in range(owners):
        source = lax.rem(me - step + owners, owners)
        if step:
            along[step - 1].wait_recv()
        piece = land.at[0, source] if step else x_ref.at[me]
        for turn in range(1, groups):
            copy = pltpu.make_async_remote_copy(
                src_ref=piece,
                dst_ref=land.at[turn, source],
                send_sem=csend.at[turn - 1, step],
                recv_sem=crecv.at[turn - 1, step],
                device_id={"cam": lax.rem(group - turn + groups, groups)},
                device_id_type=MESH,
            )
            copy.start()
            across.append((turn, source, copy))
        out_ref[0, source] = land[0, source] if step else x_ref[me]
    for turn, source, copy in across:
        copy.wait_recv()
        out_ref[turn, source] = land[turn, source]
    for copy in along:
        copy.wait_send()
    for _, _, copy in across:
        copy.wait_send()


def return_home(x, groups):
    owners = x.shape[0]
    shape = (groups,) + x.shape
    return pl.pallas_call(
        functools.partial(return_kernel, owners, groups),
        out_shape=jax.ShapeDtypeStruct(shape, F32),
        in_specs=[VMEM],
        out_specs=VMEM,
        scratch_shapes=[
            pltpu.VMEM(shape, F32),
            pltpu.SemaphoreType.DMA((owners - 1,)),
            pltpu.SemaphoreType.DMA((owners - 1,)),
            pltpu.SemaphoreType.DMA((groups - 1, owners)),
            pltpu.SemaphoreType.DMA((groups - 1, owners)),
        ],
        compiler_params=pltpu.CompilerParams(
            collective_id=7, has_side_effects=True, vmem_limit_bytes=BIG
        ),
        name="return_home",
    )(x)


def shape_of(raw):
    turn_x = jnp.tanh(raw[0])
    turn_y = jnp.tanh(raw[1])
    conic_a = 0.02 + 0.1 * softplus(raw[2])
    conic_c = 0.02 + 0.1 * softplus(raw[4])
    turn_b = jnp.tanh(raw[3])
    root = jnp.sqrt(conic_a * conic_c)
    return turn_x, turn_y, conic_a, conic_c, turn_b, root


def render_kernel(
    slot_ref, count_ref, received_ref, target_ref, image_ref, back_ref,
    feats, grads, weights, pairs, ratios, carry, before, after_tri, cot_rows, cot_cols, picture,
):
    cameras, tiles, _ = slot_ref.shape
    owners, rows, splats = received_ref.shape
    cap = rows // (PROJ * cameras)
    centre = 0.5 * TSIDE
    spread = 0.375 * TSIDE
    pixels = TSIDE * TSIDE
    half = 128
    per_chunk = half // TSIDE

    feats[...] = jnp.zeros(feats.shape, F32)
    grads[...] = jnp.zeros(grads.shape, F32)
    for index in range(cameras * cap):
        raw = [received_ref[:, index * PROJ + k, :] for k in range(PROJ)]
        turn_x, turn_y, conic_a, conic_c, turn_b, root = shape_of(raw)
        conic_b = 0.9 * root * turn_b
        feats[:, index, 0, :] = centre + spread * turn_x
        feats[:, index, 1, :] = centre + spread * turn_y
        feats[:, index, 2, :] = (0.5 * LOG2E) * conic_a
        feats[:, index, 3, :] = LOG2E * conic_b
        feats[:, index, 4, :] = (0.5 * LOG2E) * conic_c
        feats[:, index, 5, :] = math.log2(0.99) - LOG2E * softplus(6.0 - raw[5])
        for k in range(3):
            feats[:, index, 8 + k, :] = sigmoid(raw[6 + k])

    row = lax.broadcasted_iota(jnp.int32, (splats, splats), 0)
    column = lax.broadcasted_iota(jnp.int32, (splats, splats), 1)
    ones = jnp.ones((splats, splats), BF16)
    lower = jnp.where(row < column, 1.0, 0.0).astype(BF16)
    upper = jnp.where(row > column, 1.0, 0.0).astype(BF16)
    for part in range(2):
        before[part * splats : (part + 1) * splats, :splats] = lower
        before[part * splats : (part + 1) * splats, splats:] = ones
        after_tri[part * splats : (part + 1) * splats, :splats] = upper
        after_tri[part * splats : (part + 1) * splats, splats:] = ones
    grid = lax.broadcasted_iota(jnp.int32, (TSIDE, splats), 0).astype(F32) + 0.5
    pad_rows = jnp.zeros((8, splats), F32)

    def entry_of(camera, tile, position):
        slot = slot_ref[camera, tile, position]
        return slot // cap, camera * cap + slot % cap

    def tile_step(number, _):
        camera = number // tiles
        tile = number % tiles
        live = count_ref[camera, tile]
        carry[...] = jnp.zeros(carry.shape, F32)
        picture[...] = jnp.zeros(picture.shape, F32)

        def forward(pair, _):
            places = [PAIR * pair + sub for sub in range(PAIR)]
            alphas, logs, sums, shades = [], [], [], []
            for place in places:
                owner, index = entry_of(camera, tile, jnp.minimum(place, live - 1))
                part = lambda k: feats[owner, index, k : k + 1, :]
                off_x = grid - part(0)
                off_y = grid - part(1)
                in_x = -(part(2) * off_x * off_x)
                cross = -(part(3) * off_x)
                faint = jnp.where(place < live, part(5), -1e30)
                in_y = faint - part(4) * off_y * off_y
                for chunk in range(pixels // half):
                    lines = []
                    for line in range(chunk * per_chunk, (chunk + 1) * per_chunk):
                        lines.append(
                            in_x + (in_y[line : line + 1] + cross * off_y[line : line + 1])
                        )
                    alpha = jnp.exp2(jnp.concatenate(lines, axis=0))
                    log_keep = jnp.log2(1.0 - alpha)
                    alphas.append(alpha)
                    logs.append(log_keep)
                    sums.append(dot32(jnp.concatenate(split2(log_keep), axis=1), before[...]))
                colour_high, colour_low = split2(feats[owner, index, 8:16, :])
                colour_high = colour_high.astype(F32)
                colour_low = colour_low.astype(F32)
                shades.append(
                    jnp.concatenate(
                        [
                            jnp.concatenate([colour_high, colour_low], axis=0),
                            jnp.concatenate([colour_high, pad_rows], axis=0),
                        ],
                        axis=1,
                    ).astype(BF16)
                )
            chunks = pixels // half
            for chunk in range(chunks):
                where = slice(chunk * half, (chunk + 1) * half)
                held = carry[where, :]
                drawn = jnp.zeros((16, half), F32)
                for sub, place in enumerate(places):
                    at = sub * chunks + chunk
                    weight = alphas[at] * jnp.exp2(sums[at][:, :splats] + held)
                    held = held + sums[at][:, splats:]
                    both = jnp.concatenate(split2(weight), axis=1)
                    weights[place, where, :] = weight
                    pairs[place, where, :] = both
                    ratios[place, where, :] = alphas[at] * jnp.exp2(-logs[at])
                    drawn += dot32(shades[sub], both, (((1,), (1,)), ((), ())))
                carry[where, :] = held
                picture[:, where] += drawn[:8] + drawn[8:]
            return 0

        steps = (live + PAIR - 1) // PAIR
        lax.fori_loop(0, steps, forward, 0)
        for k in range(3):
            colour = picture[k : k + 1, :]
            image_ref[camera, k, pl.ds(tile, 1), :] = colour
            picture[k : k + 1, :] = LOSS_WEIGHT * (
                colour - target_ref[camera, k, pl.ds(tile, 1), :]
            )
        cot_high, cot_low = split2(picture[...])
        cot_high = cot_high.astype(F32)
        cot_low = cot_low.astype(F32)
        cot_rows[...] = jnp.concatenate([cot_high, cot_low], axis=0).astype(BF16)
        stacked = jnp.concatenate(
            [cot_high, cot_low, cot_high, jnp.zeros((half - 24, pixels), F32)], axis=0
        )
        cot_cols[...] = stacked.T.astype(BF16)
        carry[...] = jnp.zeros(carry.shape, F32)

        def backward(reverse, _):
            places = [PAIR * (steps - 1 - reverse) + PAIR - 1 - sub for sub in range(PAIR)]
            chunks = pixels // half
            spots, offsets, shaded, sums = [], [], [], []
            for place in places:
                owner, index = entry_of(camera, tile, jnp.minimum(place, live - 1))
                spots.append((owner, index))
                offsets.append(
                    (grid - feats[owner, index, 0:1, :], grid - feats[owner, index, 1:2, :])
                )
                colour_high, colour_low = split2(feats[owner, index, 8:16, :])
                colour_high = colour_high.astype(F32)
                shades = jnp.concatenate(
                    [
                        colour_high,
                        colour_high,
                        colour_low.astype(F32),
                        jnp.zeros((half - 24, splats), F32),
                    ],
                    axis=0,
                ).astype(BF16)
                for chunk in range(chunks):
                    where = slice(chunk * half, (chunk + 1) * half)
                    piece = dot32(cot_cols[where, :], shades) * weights[place, where, :]
                    shaded.append(piece)
                    sums.append(dot32(jnp.concatenate(split2(piece), axis=1), after_tri[...]))
            totals = [[jnp.zeros((TSIDE, splats), F32)] * 3 for _ in places]
            for chunk in range(chunks):
                where = slice(chunk * half, (chunk + 1) * half)
                held = carry[where, :]
                for sub, place in enumerate(places):
                    at = sub * chunks + chunk
                    pull = shaded[at] - (sums[at][:, :splats] + held) * ratios[place, where, :]
                    held = held + sums[at][:, splats:]
                    total0, total1, total2 = totals[sub]
                    off_y = offsets[sub][1]
                    for line in range(per_chunk):
                        height = off_y[chunk * per_chunk + line : chunk * per_chunk + line + 1]
                        piece = pull[line * TSIDE : (line + 1) * TSIDE]
                        lifted = piece * height
                        total0 += piece
                        total1 += lifted
                        total2 += lifted * height
                    totals[sub] = [total0, total1, total2]
                carry[where, :] = held
            sum_of = lambda value: jnp.sum(value, axis=0, keepdims=True)
            for sub, place in enumerate(places):
                owner, index = spots[sub]
                total0, total1, total2 = totals[sub]
                off_x = offsets[sub][0]
                wide = total0 * off_x
                moments = jnp.concatenate(
                    [
                        sum_of(total0),
                        sum_of(wide),
                        sum_of(total1),
                        sum_of(wide * off_x),
                        sum_of(total1 * off_x),
                        sum_of(total2),
                        jnp.zeros((2, splats), F32),
                    ],
                    axis=0,
                )
                tinted = dot32(cot_rows[...], pairs[place])
                grads[owner, index, 0:8, :] += moments
                grads[owner, index, 8:16, :] += (
                    tinted[:8, :splats] + tinted[8:, :splats] + tinted[:8, splats:]
                )
            return 0

        lax.fori_loop(0, steps, backward, 0)
        return 0

    lax.fori_loop(0, cameras * tiles, tile_step, 0)

    for index in range(cameras * cap):
        raw = [received_ref[:, index * PROJ + k, :] for k in range(PROJ)]
        turn_x, turn_y, conic_a, conic_c, turn_b, root = shape_of(raw)
        conic_b = 0.9 * root * turn_b
        sum0, sum_x, sum_y, sum_xx, sum_xy, sum_yy = [grads[:, index, k, :] for k in range(6)]
        grad_b = -sum_xy
        grad_a = -0.5 * sum_xx + grad_b * (0.5 * conic_b / conic_a)
        grad_c = -0.5 * sum_yy + grad_b * (0.5 * conic_b / conic_c)
        results = [
            (conic_a * sum_x + conic_b * sum_y) * (spread * (1.0 - turn_x * turn_x)),
            (conic_b * sum_x + conic_c * sum_y) * (spread * (1.0 - turn_y * turn_y)),
            grad_a * (0.1 * sigmoid(raw[2])),
            grad_b * (0.9 * root * (1.0 - turn_b * turn_b)),
            grad_c * (0.1 * sigmoid(raw[4])),
            sum0 * sigmoid(6.0 - raw[5]),
        ]
        for k in range(3):
            tone = sigmoid(raw[6 + k])
            results.append(grads[:, index, 8 + k, :] * (tone * (1.0 - tone)))
        for k in range(PROJ):
            back_ref[:, index * PROJ + k, :] = results[k]


def render(slots, counts, received, targets):
    owners, rows, splats = received.shape
    cameras, tiles, depth = slots.shape
    pixels = targets.shape[-1]
    cap = rows // (PROJ * cameras)
    depth = -(-depth // PAIR) * PAIR
    return pl.pallas_call(
        render_kernel,
        out_shape=(
            jax.ShapeDtypeStruct(targets.shape, F32),
            jax.ShapeDtypeStruct(received.shape, F32),
        ),
        in_specs=[SMEM, SMEM, VMEM, VMEM],
        out_specs=(VMEM, VMEM),
        scratch_shapes=[
            pltpu.VMEM((owners, cameras * cap, 16, splats), F32),
            pltpu.VMEM((owners, cameras * cap, 16, splats), F32),
            pltpu.VMEM((depth, pixels, splats), F32),
            pltpu.VMEM((depth, pixels, 2 * splats), BF16),
            pltpu.VMEM((depth, pixels, splats), F32),
            pltpu.VMEM((pixels, splats), F32),
            pltpu.VMEM((2 * splats, 2 * splats), BF16),
            pltpu.VMEM((2 * splats, 2 * splats), BF16),
            pltpu.VMEM((16, pixels), BF16),
            pltpu.VMEM((pixels, 128), BF16),
            pltpu.VMEM((8, pixels), F32),
        ],
        compiler_params=pltpu.CompilerParams(vmem_limit_bytes=BIG),
        cost_estimate=pl.CostEstimate(
            flops=20_000_000_000, bytes_accessed=100_000_000, transcendentals=4_000_000
        ),
        name="render",
    )(slots, counts, received, targets)


def update_kernel(groups, *refs):
    send_ref, split_ref, live_ref, back_ref, params_ref = refs[:5]
    packs = refs[5 : 5 + groups]
    params_out, first_out, second_out, parent_out, table, slopes = refs[5 + groups :]
    me = lax.axis_index("cam")
    owners, rows = back_ref.shape[1:3]
    values, share, splats = first_out.shape
    cameras = table.shape[1] // (16 * groups)
    cap = rows // (PROJ * cameras)
    table[...] = jnp.zeros(table.shape, F32)
    for turn in range(groups):
        for owner in range(owners):
            for camera in range(cameras):
                for place in range(cap):
                    block = send_ref[turn, (camera * cap + place) * owners + owner]
                    first = (camera * cap + place) * PROJ
                    into = (turn * cameras + camera) * 16
                    table[block, into : into + PROJ, :] += back_ref[
                        turn, owner, first : first + PROJ, :
                    ]
    held = values * share
    stacked = jnp.concatenate(
        [pack[2 * held : 2 * held + 16 * cameras, :] for pack in packs], axis=0
    )
    matrix_high, matrix_low = split2(stacked.T[: -(-values // 16) * 16])
    both = jnp.concatenate([matrix_high, matrix_low], axis=1)
    for turn in range(groups):
        base = pl.multiple_of(lax.rem(me + turn, groups) * share, share)
        for place in range(share):
            high, low = split2(table[base + place])
            gradient = dot32(both, jnp.concatenate([high, high], axis=0)) + dot32(matrix_high, low)
            slopes[:, place, :] = gradient[:values]
        pack = packs[turn]
        for start in range(0, values, 8):
            end = min(values, start + 8)
            size = (end - start, share, splats)
            gradient = slopes[start:end]
            first = pack[start * share : end * share, :].reshape(size)
            second = pack[held + start * share : held + end * share, :].reshape(size)
            new_first = BETA_FIRST * first + (1.0 - BETA_FIRST) * gradient
            new_second = BETA_SECOND * second + (1.0 - BETA_SECOND) * gradient * gradient
            params_out[start:end, pl.ds(base, share), :] = params_ref[
                start:end, pl.ds(base, share), :
            ] - RATE * new_first / (jnp.sqrt(new_second) + EPSILON)
            if turn == 0:
                first_out[start:end] = new_first
                second_out[start:end] = new_second
    for owner in range(split_ref.shape[1]):
        alive = live_ref[0, owner].astype(F32)
        chosen = params_out[:, pl.ds(split_ref[0, owner], 1), :].reshape(values, splats)
        parent_out[owner, 0:values, :] = chosen * alive
        parent_out[owner, values : values + 1, :] = jnp.zeros((1, splats), F32) + alive


def update(sends, split_block, split_live, back, params, packs, share, cameras):
    groups = len(packs)
    values, owned, splats = params.shape
    moments = jax.ShapeDtypeStruct((values, share, splats), F32)
    return pl.pallas_call(
        functools.partial(update_kernel, groups),
        out_shape=(
            jax.ShapeDtypeStruct(params.shape, F32),
            moments,
            moments,
            jax.ShapeDtypeStruct((split_block.shape[1], values + 1, splats), F32),
        ),
        in_specs=[SMEM, SMEM, SMEM] + [VMEM] * (2 + groups),
        out_specs=(VMEM,) * 4,
        scratch_shapes=[
            pltpu.VMEM((owned, groups * 16 * cameras, splats), F32),
            pltpu.VMEM((values, share, splats), F32),
        ],
        compiler_params=pltpu.CompilerParams(vmem_limit_bytes=BIG),
        name="update",
    )(sends, split_block, split_live, back, params, *packs)


def divide_kernel(parent_ref, child_ref):
    values = parent_ref.shape[1] - 1
    line = lax.broadcasted_iota(jnp.int32, (values, parent_ref.shape[2]), 0)
    for owner in range(parent_ref.shape[0]):
        alive = parent_ref[owner, values : values + 1, :]
        parent = parent_ref[owner, 0:values, :]
        shift = jnp.concatenate(
            [
                0.5 * jnp.exp(parent[3:6] - 1.0) * alive,
                jnp.zeros((values - 3, parent.shape[1]), F32),
            ],
            axis=0,
        )
        shrunk = parent - jnp.where((line >= 3) & (line < 6), SHRINK, 0.0) * alive
        child_ref[owner, :, 0, :] = shrunk + shift
        child_ref[owner, :, 1, :] = shrunk - shift


def divide(parents):
    owners, rows, splats = parents.shape
    return pl.pallas_call(
        divide_kernel,
        out_shape=jax.ShapeDtypeStruct((owners, rows - 1, 2, splats), F32),
        in_specs=[VMEM],
        out_specs=VMEM,
        compiler_params=pltpu.CompilerParams(vmem_limit_bytes=BIG),
        name="divide",
    )(parents)


def body(
    params, moment_first, moment_second, cam_proj, send_block,
    tile_slot, tile_count, targets, split_block, split_live,
):
    groups = lax.axis_size("cam")
    cameras, rows, values = cam_proj.shape
    owned, _, splats = params.shape
    share = moment_first.shape[2]
    matrix = jnp.pad(cam_proj, ((0, 0), (0, 16 - rows), (0, 128 - values)))
    matrix = matrix.reshape(cameras * 16, 128)
    send_block = send_block.transpose(0, 1, 3, 2)
    numbers = send_block.astype(F32).reshape(-1)
    numbers = jnp.pad(numbers, (0, -numbers.size % 1024)).reshape(-1, 128)
    by_value = lambda moment: moment[0, 0].transpose(1, 0, 2).reshape(values * share, splats)
    pack = jnp.concatenate([by_value(moment_first), by_value(moment_second), matrix, numbers])
    packs = [pack]
    for turn in range(1, groups):
        pattern = [((one + turn) % groups, one) for one in range(groups)]
        packs.append(lax.ppermute(pack, "cam", pattern))
    first_number = 2 * values * share + cameras * 16
    used = -(-send_block.size // 128)
    sends = jnp.stack([one[first_number : first_number + used].reshape(-1) for one in packs])
    sends = sends.astype(jnp.int32)

    by_block = params.transpose(1, 0, 2)
    received = project(send_block, matrix, by_block)
    images, back = render(tile_slot, tile_count, received, targets.transpose(0, 2, 1, 3))
    gathered = return_home(back, groups)
    new_params, new_first, new_second, parents = update(
        sends, split_block, split_live, gathered, by_block, packs, share, cameras
    )
    children = divide(exchange(parents, "dev", 6))
    restore = lambda moment: moment.transpose(1, 0, 2).reshape(moment_first.shape)
    return (
        images.transpose(0, 2, 1, 3),
        new_params.transpose(1, 0, 2),
        restore(new_first),
        restore(new_second),
        children.transpose(0, 2, 1, 3),
    )


def solution(mesh):
    placed = (
        P("dev", None, None),
        P("dev", "cam", None, None, None),
        P("dev", "cam", None, None, None),
        P("cam", None, None),
        P("cam", "dev", None, None),
        P("cam", "dev", None),
        P("cam", "dev"),
        P("cam", "dev", None, None),
        P("dev", None),
        P("dev", None),
    )
    return jax.shard_map(
        body,
        mesh=mesh,
        in_specs=placed,
        out_specs=(
            P("cam", "dev", None, None),
            P("dev", None, None),
            P("dev", "cam", None, None, None),
            P("dev", "cam", None, None, None),
            P("dev", None, None, None),
        ),
        check_vma=False,
    )
```
